32 devices in a mesh: leaf: 8 (over z, x), panel: 4 (over y, core).
Axes of the slice: x: 2, y: 2, z: 4, core: 2. Of those that a mesh axis runs over, the one named last changes fastest.
Arguments:
- leaf_sides: bfloat16 [16384, 128], P(('leaf', 'panel')), may hold values from -6 to 6
- leaf_inverse: bfloat16 [16384, 2048], P(('leaf', 'panel')), may hold values from -0.1875 to 0.1875
- leaf_panels: bfloat16 [3, 4096, 16384], P(None, 'panel', 'leaf'), may hold values from -0.125 to 0.125
- parent_map: int32 [8], P('leaf'), may hold values from 0 to 3, as said below
- tile_mask: int32 [8, 3, 32], P('leaf'), may hold values 0 or 1
- top_sides: bfloat16 [7, 4096, 128], P(None, ('panel', 'leaf')), may hold values from -6 to 6
- grand_inverse: bfloat16 [16384, 4096], P('leaf', 'panel'), may hold values from -0.125 to 0.125
- child_inverse: bfloat16 [8192, 4096], P('leaf', 'panel'), may hold values from -0.125 to 0.125
- root_inverse: bfloat16 [4096, 4096], P('leaf', 'panel'), may hold values from -0.125 to 0.125
- child_panels: bfloat16 [4096, 16384], P('panel', 'leaf'), may hold values from -0.09375 to 0.09375
- root_grand: bfloat16 [4096, 16384], P('panel', 'leaf'), may hold values from -0.09375 to 0.09375
- root_child: bfloat16 [4096, 8192], P('panel', 'leaf'), may hold values from -0.09375 to 0.09375
Outputs:
- leaf_solution: bfloat16 [16384, 128], P(('leaf', 'panel'))
- top_solution: bfloat16 [7, 4096, 128], P(None, ('panel', 'leaf'))
The draws below stay inside these ranges and needn't reach their ends.
Inputs may be any that keep to these rules, and one draw needn't show every extreme that they name: `parent_map`: each of the 4 grandchild separators is the parent of at least one subtree.
All inputs are finite; a program needn't handle non-finite values. No bound on the sum of `tile_mask` on one device may be relied on, other than what follows from the above.
Results may differ from the reference program's by a relative error of at most 0.017.
Values may be sent and summed in bfloat16 or wider, within the bound.
No kernel may reach another device: no remote copies, remote signals or barrier semaphores. Data moves between devices by JAX's collectives and lax.ppermute only.
A program may use at most 128 MiB of HBM per device.

```python
import jax
import jax.numpy as jnp
from jax import lax

S = 4096
W = 2048
R = 128
TILE_ROWS = 128
SUBTREES = 8


def draw_parent_map(key, part):
    key_labels = jax.random.fold_in(key, 101)
    key_first = jax.random.fold_in(key, 202)
    key_second = jax.random.fold_in(key, 303)
    key_order = jax.random.fold_in(key, 404)
    labels = jax.random.permutation(key_labels, jnp.arange(4, dtype=jnp.int32))
    first_pick = jax.random.randint(key_first, (SUBTREES,), 0, 4, dtype=jnp.int32)
    second_pick = jax.random.randint(key_second, (SUBTREES,), 0, 4, dtype=jnp.int32)
    ranked = jnp.minimum(first_pick, second_pick)
    ranked = ranked.at[0:4].set(jnp.arange(4, dtype=jnp.int32))
    shuffled = jax.random.permutation(key_order, jnp.arange(SUBTREES, dtype=jnp.int32))
    return labels[ranked[shuffled]].astype(jnp.int32)


def set_ends(result, own_key, least, largest):
    longest = result.shape.index(max(result.shape))
    spots = []
    for shift in (0, 1):
        where = [jax.random.randint(jax.random.fold_in(own_key, axis), (), 0, length) for axis, length in enumerate(result.shape)]
        where[longest] = (where[longest] + shift) % result.shape[longest]
        spots.append(tuple(where))
    return result.at[spots[0]].set(least).at[spots[1]].set(largest)


def steps_of(rng, dims, shards, low, top_value):
    def one(axis_at, shards_of):
        heights = jax.random.uniform(jax.random.fold_in(jax.random.fold_in(rng, 6), axis_at), (shards_of,), jnp.float32, low / len(shards), top_value / len(shards))
        return jnp.repeat(jnp.exp(heights), dims[axis_at] // shards_of).reshape((-1,) + (1,) * (len(dims) - axis_at - 1))

    gain = one(*shards[0])
    for cut in shards[1:]:
        gain = gain * one(*cut)
    return gain


def normal_values(own_key, extent, deviation, limit, pieces=(), held_as=jnp.bfloat16):
    result = deviation * jax.random.normal(own_key, extent, jnp.float32)
    if pieces:
        result = result * steps_of(own_key, extent, pieces, -0.22, 0.18)
    return jnp.clip(result, -limit, limit).astype(held_as)


def setup_inputs(seed: int = 0) -> dict:
    splits = jax.random.split(jax.random.key(seed), 13)
    return {
        "leaf_sides": normal_values(splits[0], (SUBTREES * W, R), 1.0, 6.0, ((0, 32),)),
        "leaf_inverse": normal_values(splits[1], (SUBTREES * W, W), (W // 2) ** -0.5, 0.1875, ((0, 32),)),
        "leaf_panels": normal_values(splits[2], (3, S, SUBTREES * W), W ** -0.5, 0.125, ((1, 4), (2, 8))),
        "parent_map": draw_parent_map(jax.random.fold_in(splits[12], 71), 0),
        "tile_mask": set_ends((jax.random.randint(splits[4], (SUBTREES, 3, S // TILE_ROWS), 0, 2) < 1).astype(jnp.int32), jax.random.fold_in(splits[4], 1), 0, 1),
        "top_sides": normal_values(splits[5], (7, S, R), 1.0, 6.0, ((1, 32),)),
        "grand_inverse": normal_values(splits[6], (4 * S, S), (S // 2) ** -0.5, 0.125, ((0, 8), (1, 4))),
        "child_inverse": normal_values(splits[7], (2 * S, S), (S // 2) ** -0.5, 0.125, ((0, 8), (1, 4))),
        "root_inverse": normal_values(splits[8], (S, S), (S // 2) ** -0.5, 0.125, ((0, 8), (1, 4))),
        "child_panels": normal_values(splits[9], (S, 4 * S), S ** -0.5, 0.09375, ((0, 4), (1, 8))),
        "root_grand": normal_values(splits[10], (S, 4 * S), S ** -0.5, 0.09375, ((0, 4), (1, 8))),
        "root_child": normal_values(splits[11], (S, 2 * S), S ** -0.5, 0.09375, ((0, 4), (1, 8))),
    }


def lower_block(matrix, first_row, count):
    return jnp.tril(lax.dynamic_slice_in_dim(matrix, first_row, count, 0))


def reference(leaf_sides, leaf_inverse, leaf_panels, parent_map, tile_mask, top_sides, grand_inverse, child_inverse, root_inverse, child_panels, root_grand, root_child):
    subtrees = parent_map.shape[0]
    leaf_width = leaf_inverse.shape[1]
    separator = root_inverse.shape[0]
    side_count = leaf_sides.shape[1]
    subtree_list = jnp.arange(subtrees, dtype=jnp.int32)

    def expand_mask(subtree):
        tile_flags = lax.dynamic_index_in_dim(tile_mask, subtree, 0, keepdims=False).astype(jnp.float32)
        return jnp.repeat(tile_flags, TILE_ROWS, axis=1)

    def forward(running, subtree):
        first_row = subtree * leaf_width
        right_sides = lax.dynamic_slice_in_dim(leaf_sides, first_row, leaf_width, 0)
        triangle = lower_block(leaf_inverse, first_row, leaf_width)
        solved = jnp.dot(triangle, right_sides, preferred_element_type=jnp.float32).astype(jnp.bfloat16)
        panels = lax.dynamic_slice_in_dim(leaf_panels, first_row, leaf_width, 2)
        updates = jnp.stack([jnp.dot(panels[ancestor], solved, preferred_element_type=jnp.float32) for ancestor in range(3)])
        updates = updates * expand_mask(subtree)[:, :, None]
        parent = lax.dynamic_index_in_dim(parent_map, subtree, 0, keepdims=False)
        grand_slots = (jnp.arange(4, dtype=jnp.int32) == parent).astype(jnp.float32)
        child_slots = (jnp.arange(2, dtype=jnp.int32) == parent // 2).astype(jnp.float32)
        grand_sum, child_sum, root_sum = running
        return (grand_sum + grand_slots[:, None, None] * updates[0][None], child_sum + child_slots[:, None, None] * updates[1][None], root_sum + updates[2]), solved

    initial = (jnp.zeros((4, separator, side_count), jnp.float32), jnp.zeros((2, separator, side_count), jnp.float32), jnp.zeros((separator, side_count), jnp.float32))
    (grand_leaf, child_leaf, root_leaf), leaf_solved = lax.scan(forward, initial, subtree_list)

    top_right = top_sides.astype(jnp.float32)
    grand_lower = [jnp.tril(grand_inverse[slot * separator:(slot + 1) * separator]) for slot in range(4)]
    child_lower = [jnp.tril(child_inverse[slot * separator:(slot + 1) * separator]) for slot in range(2)]
    root_lower = jnp.tril(root_inverse)

    grand_solved = []
    for slot in range(4):
        grand_right = (top_right[slot] - grand_leaf[slot]).astype(jnp.bfloat16)
        grand_solved.append(jnp.dot(grand_lower[slot], grand_right, preferred_element_type=jnp.float32).astype(jnp.bfloat16))
    child_solved = []
    for slot in range(2):
        child_right = top_right[4 + slot] - child_leaf[slot]
        for grand_slot in (2 * slot, 2 * slot + 1):
            child_right = child_right - jnp.dot(child_panels[:, grand_slot * separator:(grand_slot + 1) * separator], grand_solved[grand_slot], preferred_element_type=jnp.float32)
        child_solved.append(jnp.dot(child_lower[slot], child_right.astype(jnp.bfloat16), preferred_element_type=jnp.float32).astype(jnp.bfloat16))
    root_right = top_right[6] - root_leaf
    for slot in range(4):
        root_right = root_right - jnp.dot(root_grand[:, slot * separator:(slot + 1) * separator], grand_solved[slot], preferred_element_type=jnp.float32)
    for slot in range(2):
        root_right = root_right - jnp.dot(root_child[:, slot * separator:(slot + 1) * separator], child_solved[slot], preferred_element_type=jnp.float32)
    root_solved = jnp.dot(root_lower, root_right.astype(jnp.bfloat16), preferred_element_type=jnp.float32).astype(jnp.bfloat16)

    root_result = jnp.dot(root_lower.T, root_solved, preferred_element_type=jnp.float32).astype(jnp.bfloat16)
    child_result = []
    for slot in range(2):
        residual = child_solved[slot].astype(jnp.float32) - jnp.dot(root_child[:, slot * separator:(slot + 1) * separator].T, root_result, preferred_element_type=jnp.float32)
        child_result.append(jnp.dot(child_lower[slot].T, residual.astype(jnp.bfloat16), preferred_element_type=jnp.float32).astype(jnp.bfloat16))
    grand_result = []
    for slot in range(4):
        residual = grand_solved[slot].astype(jnp.float32)
        residual = residual - jnp.dot(child_panels[:, slot * separator:(slot + 1) * separator].T, child_result[slot // 2], preferred_element_type=jnp.float32)
        residual = residual - jnp.dot(root_grand[:, slot * separator:(slot + 1) * separator].T, root_result, preferred_element_type=jnp.float32)
        grand_result.append(jnp.dot(grand_lower[slot].T, residual.astype(jnp.bfloat16), preferred_element_type=jnp.float32).astype(jnp.bfloat16))
    grand_stack = jnp.stack(grand_result)
    child_stack = jnp.stack(child_result)

    def backward(running, subtree):
        first_row = subtree * leaf_width
        parent = lax.dynamic_index_in_dim(parent_map, subtree, 0, keepdims=False)
        ancestors = jnp.stack([lax.dynamic_index_in_dim(grand_stack, parent, 0, keepdims=False), lax.dynamic_index_in_dim(child_stack, parent // 2, 0, keepdims=False), root_result])
        ancestors = ancestors * expand_mask(subtree)[:, :, None].astype(jnp.bfloat16)
        panels = lax.dynamic_slice_in_dim(leaf_panels, first_row, leaf_width, 2)
        pulled = sum([jnp.dot(panels[ancestor].T, ancestors[ancestor], preferred_element_type=jnp.float32) for ancestor in range(3)])
        solved = lax.dynamic_index_in_dim(leaf_solved, subtree, 0, keepdims=False)
        residual = (solved.astype(jnp.float32) - pulled).astype(jnp.bfloat16)
        triangle = lower_block(leaf_inverse, first_row, leaf_width)
        return running, jnp.dot(triangle.T, residual, preferred_element_type=jnp.float32).astype(jnp.bfloat16)

    unused, leaf_result = lax.scan(backward, jnp.zeros((), jnp.float32), subtree_list)
    leaf_solution = leaf_result.reshape(subtrees * leaf_width, side_count)
    top_solution = jnp.concatenate([grand_stack, child_stack, root_result[None]], axis=0)
    return leaf_solution, top_solution
```

```python
import jax
import jax.numpy as jnp
from jax import lax
from jax.sharding import Mesh
from jax.sharding import PartitionSpec as P

TILE_ROWS = 128
LEAF = ("c", "g", "h")
PANEL = ("y", "k")
DEPTH = ("c", "g")
F32 = jnp.float32
BF16 = jnp.bfloat16


def lower_part(matrix, row_offset, col_offset):
    row_index = row_offset + lax.broadcasted_iota(jnp.int32, matrix.shape, 0)
    col_index = col_offset + lax.broadcasted_iota(jnp.int32, matrix.shape, 1)
    return jnp.where(row_index >= col_index, matrix, jnp.zeros_like(matrix))


def product(matrix, vectors):
    return jnp.dot(matrix, vectors, preferred_element_type=F32)


def transpose_product(matrix, vectors):
    return lax.dot_general(
        matrix, vectors, (((0,), (0,)), ((), ())), preferred_element_type=F32
    )


def rows_at(value, start, count):
    return lax.dynamic_slice_in_dim(value, start, count, 0)


def shift(value, axis, step):
    size = lax.axis_size(axis)
    return lax.ppermute(value, axis, [(i, (i + step) % size) for i in range(size)])


def add_others(own, sent, axis):
    for step in range(1, lax.axis_size(axis)):
        own = own + shift(sent, axis, step).astype(F32)
    return own


def split_sum(partial_value, axis):
    size = lax.axis_size(axis)
    index = lax.axis_index(axis)
    count = partial_value.shape[0] // size
    total = rows_at(partial_value, index * count, count)
    for step in range(1, size):
        chunk = rows_at(partial_value, (index + step) % size * count, count)
        total = total + shift(chunk.astype(BF16), axis, step).astype(F32)
    return total


def joined(piece, axis):
    size = lax.axis_size(axis)
    index = lax.axis_index(axis)
    place = lax.broadcasted_iota(jnp.int32, (size,) + piece.shape, 0)
    whole = jnp.broadcast_to(piece[None], place.shape)
    for step in range(1, size):
        arrived = shift(piece, axis, step)
        whole = jnp.where(place == (index - step) % size, arrived[None], whole)
    return whole.reshape((size * piece.shape[0],) + piece.shape[1:])


def panel_split_sum(partial_value):
    count = partial_value.shape[0] // lax.axis_size("k") // lax.axis_size("y")
    by_core = partial_value.reshape(lax.axis_size("y"), lax.axis_size("k"), count, -1)
    by_core = by_core.transpose(1, 0, 2, 3).reshape(partial_value.shape)
    return split_sum(split_sum(by_core, "k"), "y")


def panel_sum(partial_value):
    half = split_sum(partial_value, "k")
    half = add_others(half, half.astype(BF16), "y").astype(BF16)
    return joined(half, "k")


def depth_exchange(own, sent):
    size = lax.axis_size(DEPTH)
    for step in range(1, size):
        own = own + lax.ppermute(sent, DEPTH, [(i, i ^ step) for i in range(size)]).astype(F32)
    return own


def per_device(
    leaf_sides,
    leaf_inverse,
    leaf_panels,
    parent_map,
    tile_mask,
    top_sides,
    grand_inverse,
    child_inverse,
    root_inverse,
    child_panels,
    root_grand,
    root_child,
):
    z_index = lax.axis_index(DEPTH)
    g_index = lax.axis_index("g")
    h_index = lax.axis_index("h")
    leaf_index = lax.axis_index(LEAF)
    panel_index = lax.axis_index(PANEL)
    owners = lax.axis_size("h")
    leaf_count = lax.axis_size(LEAF)
    depth = lax.axis_size(DEPTH)
    part_rows = leaf_sides.shape[0]
    side_count = leaf_sides.shape[1]
    slice_rows = leaf_panels.shape[1]
    share_rows = top_sides.shape[1]
    half_rows = slice_rows // owners
    parent = parent_map[0]

    pieces = []
    for step in range(depth):
        target = (leaf_index % depth + step) % depth
        pair = jnp.stack(
            [
                lax.dynamic_index_in_dim(top_sides, target, 0, keepdims=False),
                lax.dynamic_index_in_dim(top_sides, 4 + target // 2, 0, keepdims=False),
            ]
        )
        pairs = [
            (i, (i % depth + step) % depth * owners + i // depth) for i in range(leaf_count)
        ]
        pieces.append(lax.ppermute(pair, LEAF, pairs))
    root_piece = lax.ppermute(
        top_sides[6], LEAF, [(i, i % depth * owners + i // depth) for i in range(leaf_count)]
    )
    place = lax.broadcasted_iota(jnp.int32, (depth,) + pieces[0].shape, 0)
    top_half = jnp.broadcast_to(pieces[0][None], place.shape)
    for step in range(1, depth):
        top_half = jnp.where(place == (z_index - step) % depth, pieces[step][None], top_half)
    grand_top = top_half[:, 0].reshape(half_rows, side_count).astype(F32)
    child_top = top_half[:, 1].reshape(half_rows, side_count).astype(F32)

    all_sides = lax.all_gather(leaf_sides, PANEL, axis=0, tiled=True)
    leaf_lower = lower_part(leaf_inverse, panel_index * part_rows, 0)
    solved_leaf = product(leaf_lower, all_sides).astype(BF16)
    all_solved = lax.all_gather(solved_leaf, PANEL, axis=0, tiled=True)

    tile_count = slice_rows // TILE_ROWS
    tile_rows = lax.dynamic_slice_in_dim(tile_mask[0], panel_index * tile_count, tile_count, 1)
    row_mask = jnp.repeat(tile_rows.astype(F32), TILE_ROWS, axis=1)[:, :, None]
    updates = [product(leaf_panels[k], all_solved) * row_mask[k] for k in range(3)]

    parents = [parent]
    for step in range(1, owners):
        parents.append(shift(parent_map, "h", step)[0])

    def gathered_by_row(value):
        found = [rows_at(value, h_index * half_rows, half_rows)]
        for step in range(1, owners):
            chunk = rows_at(value, (h_index + step) % owners * half_rows, half_rows)
            found.append(shift(chunk.astype(BF16), "h", step).astype(F32))
        return found

    halves = gathered_by_row(updates[0])

    def slot_sum(found, slots, wanted, divisor):
        return sum(
            jnp.where(slots // divisor == wanted // divisor, part, 0.0)
            for part, slots in zip(found, slots)
        )

    grand_right = grand_top - slot_sum(halves, parents, z_index, 1)
    for step in range(1, depth):
        sent = slot_sum(halves, parents, z_index ^ step, 1).astype(BF16)
        arrived = lax.ppermute(sent, DEPTH, [(i, i ^ step) for i in range(depth)])
        grand_right = grand_right - arrived.astype(F32)
    grand_right = joined(grand_right.astype(BF16), "h")

    child_halves = gathered_by_row(updates[1])
    root_half = sum(gathered_by_row(updates[2]))
    quarter = half_rows // 2

    def to_depth(target):
        child_part = slot_sum(child_halves, parents, 2 * (target // 2), 2)
        child_part = rows_at(child_part, target % 2 * quarter, quarter)
        root_part = rows_at(root_half, target * share_rows, share_rows)
        return jnp.concatenate([child_part, root_part], axis=0)

    level_sum = to_depth(z_index)
    for step in range(1, depth):
        sent = to_depth(z_index ^ step).astype(BF16)
        arrived = lax.ppermute(sent, DEPTH, [(i, i ^ step) for i in range(depth)])
        level_sum = level_sum + arrived.astype(F32)
    child_piece = rows_at(child_top, g_index * quarter, quarter) - level_sum[:quarter]
    root_piece = root_piece.astype(F32) - level_sum[quarter:]

    grand_lower = lower_part(
        grand_inverse, h_index * grand_inverse.shape[0], panel_index * slice_rows
    )
    grand_solved = panel_sum(product(grand_lower, grand_right))

    def placed(piece, start):
        blank = jnp.zeros((half_rows, side_count), F32)
        return lax.dynamic_update_slice_in_dim(blank, piece, start, 0)

    child_own = placed(child_piece, g_index * quarter) - split_sum(
        product(child_panels, grand_solved), "h"
    )
    child_right = add_others(child_own, child_own.astype(BF16), "g")
    child_right = joined(child_right.astype(BF16), "h")
    child_lower = lower_part(
        child_inverse,
        (g_index * owners + h_index) * child_inverse.shape[0],
        panel_index * slice_rows,
    )
    child_solved = panel_sum(product(child_lower, child_right))

    from_below = product(root_grand, grand_solved) + product(root_child, child_solved)
    root_own = placed(root_piece, z_index * share_rows) - split_sum(from_below, "h")
    root_right = depth_exchange(root_own, root_own.astype(BF16))
    root_right = joined(root_right.astype(BF16), "h")
    root_lower = lower_part(
        root_inverse, leaf_index * root_inverse.shape[0], panel_index * slice_rows
    )
    root_solved = panel_sum(product(root_lower, root_right))
    root_half_result = split_sum(transpose_product(root_lower, root_solved), "h")
    root_half_result = depth_exchange(root_half_result, root_half_result.astype(BF16))
    root_result = joined(root_half_result.astype(BF16), "h")

    child_residual = child_solved.astype(F32) - panel_sum(
        transpose_product(root_child, root_result)
    ).astype(F32)
    child_half = split_sum(transpose_product(child_lower, child_residual.astype(BF16)), "h")
    child_half = add_others(child_half, child_half.astype(BF16), "g").astype(BF16)
    child_result = joined(child_half, "h")

    grand_back = transpose_product(child_panels, child_result) + transpose_product(
        root_grand, root_result
    )
    grand_residual = grand_solved.astype(F32) - panel_sum(grand_back).astype(F32)
    grand_half = split_sum(
        transpose_product(grand_lower, grand_residual.astype(BF16)), "h"
    ).astype(BF16)

    grand_halves = [grand_half] + [
        lax.ppermute(grand_half, DEPTH, [(i, i ^ step) for i in range(depth)])
        for step in range(1, depth)
    ]

    def grand_half_of(slot):
        found = grand_halves[0]
        for step in range(1, depth):
            found = jnp.where(slot == z_index ^ step, grand_halves[step], found)
        return found

    place = lax.broadcasted_iota(jnp.int32, (owners, half_rows, side_count), 0)
    own_grand = jnp.broadcast_to(grand_half_of(parent)[None], place.shape)
    for step in range(1, owners):
        wanted = shift(parent_map, "h", -step)[0]
        arrived = shift(grand_half_of(wanted), "h", step)
        own_grand = jnp.where(place == (h_index - step) % owners, arrived[None], own_grand)
    own_grand = own_grand.reshape(slice_rows, side_count)
    other_child = shift(child_result, "c", 1)
    own_child = jnp.where(parent // 2 == lax.axis_index("c"), child_result, other_child)
    ancestors = [own_grand, own_child, root_result]
    narrow_mask = row_mask.astype(BF16)
    pulled = [
        transpose_product(leaf_panels[k], ancestors[k] * narrow_mask[k]) for k in range(3)
    ]
    leaf_residual = solved_leaf.astype(F32) - panel_split_sum(pulled[2] + pulled[1] + pulled[0])
    leaf_result = transpose_product(leaf_lower, leaf_residual.astype(BF16))
    leaf_solution = panel_split_sum(leaf_result).astype(BF16)

    result_pair = jnp.stack([grand_half, child_half])
    arrived = []
    for step in range(depth):
        target = (z_index - step) % depth
        block = lax.dynamic_slice_in_dim(result_pair, target * share_rows, share_rows, 1)
        pairs = [
            ((i % depth + step) % depth * owners + i // depth, i) for i in range(leaf_count)
        ]
        arrived.append(lax.ppermute(block, LEAF, pairs))
    tops = []
    for slot in range(6):
        row, source = (0, slot) if slot < 4 else (1, 2 * (slot - 4))
        found = arrived[0][row]
        for step in range(1, depth):
            here = (leaf_index % depth + step) % depth == source
            found = jnp.where(here, arrived[step][row], found)
        tops.append(found)
    tops.append(rows_at(root_result, leaf_index * share_rows, share_rows))
    return leaf_solution, jnp.stack(tops)


def solution(mesh):
    leaf_count = mesh.shape["leaf"]
    panel_count = mesh.shape["panel"]
    split_mesh = Mesh(
        mesh.devices.reshape(2, 2, leaf_count // 4, panel_count // 2, 2), LEAF + PANEL
    )
    placed = (
        P(LEAF + PANEL, None),
        P(LEAF + PANEL, None),
        P(None, PANEL, LEAF),
        P(LEAF),
        P(LEAF, None, None),
        P(None, PANEL + LEAF, None),
        P(LEAF, PANEL),
        P(LEAF, PANEL),
        P(LEAF, PANEL),
        P(PANEL, LEAF),
        P(PANEL, LEAF),
        P(PANEL, LEAF),
    )
    return jax.shard_map(
        per_device,
        mesh=split_mesh,
        in_specs=placed,
        out_specs=(P(LEAF + PANEL, None), P(None, PANEL + LEAF, None)),
        check_vma=False,
    )
```

```python
import jax
import jax.numpy as jnp
from jax import lax
from jax.experimental import pallas as pl
from jax.experimental.pallas import tpu as pltpu
from jax.sharding import Mesh
from jax.sharding import PartitionSpec as P

TILE_ROWS = 128
LANES = 128
LEAF = ("c", "g", "h")
PANEL = ("y", "k")
DEPTH = ("c", "g")
F32 = jnp.float32
BF16 = jnp.bfloat16
VMEM = pltpu.VMEM


def held(value):
    return pltpu.with_memory_space_constraint(value, VMEM)


def after(value, other):
    return lax.optimization_barrier((value, other))[0]


def lower_part(matrix, row_offset, col_offset):
    row_index = row_offset + lax.broadcasted_iota(jnp.int32, matrix.shape, 0)
    col_index = col_offset + lax.broadcasted_iota(jnp.int32, matrix.shape, 1)
    return jnp.where(row_index >= col_index, matrix, jnp.zeros_like(matrix))


def rows_at(value, start, count):
    return lax.dynamic_slice_in_dim(value, start, count, 0)


def own(value):
    return [(value, lambda: 0)]


def joined(pieces):
    if len(pieces) == 1:
        return pieces[0][0]
    count = pieces[0][0].shape[0]
    place = lax.broadcasted_iota(jnp.int32, (len(pieces),) + pieces[0][0].shape, 0)
    whole = jnp.broadcast_to(pieces[0][0][None], place.shape)
    for value, index in pieces[1:]:
        whole = jnp.where(place == index(), value[None], whole)
    return whole.reshape((len(pieces) * count,) + pieces[0][0].shape[1:])


def times(matrix, pieces, start, count, *, name, transposed=False, base=0, full=None, plus=None, scale=None, dtype=F32):
    if pieces[0][0].shape[0] % LANES:
        pieces = own(joined(pieces))
    full = full or matrix.shape[int(transposed)]
    if count % LANES and count < full:
        whole = times(
            matrix, pieces, lambda: 0, full, name=name, transposed=transposed, base=base,
            plus=plus, scale=scale, dtype=dtype,
        )
        return rows_at(whole, start(), count)
    width = pieces[0][0].shape[0]
    sides = pieces[0][0].shape[1]
    extra = [value for value in (plus, scale) if value is not None]

    def kernel(matrix_ref, *refs):
        out_ref = refs[-1]
        vector_refs = refs[: len(pieces)]
        extra_refs = list(refs[len(pieces) : -1])
        first = start()
        if count % LANES == 0:
            first = pl.multiple_of(first, LANES)
        window = pl.ds(first, count)
        total = None
        for vector_ref, (_, index) in zip(vector_refs, pieces):
            offset = index() * width
            if width % LANES == 0:
                offset = pl.multiple_of(offset, LANES)
            if transposed:
                block = matrix_ref[pl.ds(base + offset, width), window]
                part = lax.dot_general(
                    vector_ref[...], block, (((0,), (0,)), ((), ())), preferred_element_type=F32
                )
            else:
                block = matrix_ref[pl.ds(base + first, count), pl.ds(offset, width)]
                part = jnp.dot(block, vector_ref[...], preferred_element_type=F32)
            total = part if total is None else total + part
        if transposed:
            total = total.T
        if plus is not None:
            total = total + extra_refs.pop(0)[window, :].astype(F32)
        if scale is not None:
            total = total * extra_refs.pop(0)[window, :].astype(F32)
        out_ref[...] = total.astype(dtype)

    depth = len(pieces) * width
    return pl.pallas_call(
        kernel,
        out_shape=VMEM((count, sides), dtype),
        in_specs=[pl.BlockSpec(memory_space=VMEM)] * (1 + len(pieces) + len(extra)),
        out_specs=pl.BlockSpec(memory_space=VMEM),
        compiler_params=pltpu.CompilerParams(vmem_limit_bytes=6 << 20),
        cost_estimate=pl.CostEstimate(
            flops=2 * count * depth * sides,
            bytes_accessed=2 * count * depth,
            transcendentals=0,
        ),
        name=name,
    )(held(matrix), *[held(value) for value, _ in pieces], *[held(value) for value in extra])


def shift(value, axis, step):
    size = lax.axis_size(axis)
    return lax.ppermute(value, axis, [(i, (i + step) % size) for i in range(size)])


def pieces_along(value, axis):
    size = lax.axis_size(axis)
    found = [(value, lambda: lax.axis_index(axis))]
    for step in range(1, size):
        found.append(
            (shift(value, axis, step), lambda step=step: (lax.axis_index(axis) - step) % size)
        )
    return found


def split_product(product, count, axis):
    size = lax.axis_size(axis)
    arrived = []
    for step in range(1, size):
        sent = product(
            lambda step=step: (lax.axis_index(axis) + step) % size * (count // size),
            count // size,
            BF16,
        )
        arrived.append(shift(sent, axis, step))
    kept = product(lambda: lax.axis_index(axis) * (count // size), count // size, F32)
    return kept, arrived


def total_of(kept, arrived):
    for part in arrived:
        kept = kept + part.astype(F32)
    return kept


def others(value, axis):
    return [shift(value, axis, step) for step in range(1, lax.axis_size(axis))]


def panel_solve(product, count, less_from=None):
    kept, arrived = split_product(product, count, "k")
    half = total_of(kept, arrived)
    narrow = half.astype(BF16)
    half = total_of(half, others(narrow, "y"))
    if less_from is not None:
        half = less_from[0][0].astype(F32) - half
    return pieces_along(half.astype(BF16), "k")


def depth_others(value):
    size = lax.axis_size(DEPTH)
    return [
        lax.ppermute(value, DEPTH, [(i, i ^ step) for i in range(size)])
        for step in range(1, size)
    ]


def per_device(
    leaf_sides,
    leaf_inverse,
    leaf_panels,
    parent_map,
    tile_mask,
    top_sides,
    grand_inverse,
    child_inverse,
    root_inverse,
    child_panels,
    root_grand,
    root_child,
):
    z_index = lax.axis_index(DEPTH)
    g_index = lax.axis_index("g")
    h_index = lax.axis_index("h")
    leaf_index = lax.axis_index(LEAF)
    panel_index = lax.axis_index(PANEL)
    owners = lax.axis_size("h")
    depth = lax.axis_size(DEPTH)
    rows_y = lax.axis_size("y")
    part_rows = leaf_sides.shape[0]
    side_count = leaf_sides.shape[1]
    slice_rows = leaf_panels.shape[1]
    width = leaf_panels.shape[2]
    share_rows = top_sides.shape[1]
    half_rows = slice_rows // owners
    quarter = half_rows // 2
    parent = parent_map[0]
    panels = leaf_panels.reshape(3 * slice_rows, width)

    def hidx():
        return lax.axis_index("h")

    note = jnp.broadcast_to(parent.astype(BF16), (16, side_count))
    packet = jnp.concatenate([top_sides.reshape(7 * share_rows, side_count), note], axis=0)
    packets = [(packet, parent, h_index)]
    for step in range(1, owners):
        arrived = shift(packet, "h", step)
        packets.append((arrived, arrived[7 * share_rows, 0].astype(jnp.int32), (h_index - step) % owners))
    parents = [item[1] for item in packets]
    place = lax.broadcasted_iota(jnp.int32, (7, depth, share_rows, side_count), 1)
    top_part = jnp.zeros(place.shape, BF16)
    for arrived, _, source in packets:
        holder = z_index * owners + source
        block = arrived[: 7 * share_rows].reshape(7, 1, share_rows, side_count)
        here = (place == holder % depth) & (holder // depth == h_index)
        top_part = jnp.where(here, block, top_part)
    top_part = top_part.reshape(7, half_rows, side_count)

    leaf_lower = held(lower_part(leaf_inverse, panel_index * part_rows, 0))
    grand_lower = held(
        lower_part(grand_inverse, h_index * grand_inverse.shape[0], panel_index * slice_rows)
    )
    child_lower = held(
        lower_part(
            child_inverse,
            (g_index * owners + h_index) * child_inverse.shape[0],
            panel_index * slice_rows,
        )
    )
    root_lower = held(
        lower_part(root_inverse, leaf_index * root_inverse.shape[0], panel_index * slice_rows)
    )

    def panel_pieces(value):
        found = []
        for piece, place_y in pieces_along(value, "y"):
            for item, place_k in pieces_along(piece, "k"):
                found.append((item, lambda a=place_y, b=place_k: a() * 2 + b()))
        return found

    solved_leaf = times(
        leaf_lower, panel_pieces(leaf_sides), lambda: 0, part_rows, name="leaf_solve", dtype=BF16
    )
    all_solved = panel_pieces(solved_leaf)

    tile_count = slice_rows // TILE_ROWS
    tile_rows = lax.dynamic_slice_in_dim(tile_mask[0], panel_index * tile_count, tile_count, 1)
    row_mask = jnp.broadcast_to(
        tile_rows.astype(BF16)[:, :, None, None], (3, tile_count, TILE_ROWS, side_count)
    ).reshape(3, slice_rows, side_count)

    def update(level, pieces, name):
        def product(start, count, dtype):
            return times(
                panels, pieces, start, count, name=name, base=level * slice_rows,
                full=slice_rows, scale=row_mask[level], dtype=dtype,
            )

        return split_product(product, slice_rows, "h")

    def slot_sum(found, wanted, divisor):
        return sum(
            jnp.where(slot // divisor == wanted // divisor, part.astype(F32), 0.0)
            for part, slot in zip(found, parents)
        )

    kept, arrived = update(0, all_solved, "grand_update")
    halves = [kept] + arrived

    def grand_slot(target):
        top = lax.dynamic_index_in_dim(top_part, target, 0, keepdims=False).astype(F32)
        return top - slot_sum(halves, target, 1)

    sent = [grand_slot(z_index ^ step).astype(BF16) for step in range(1, depth)]
    grand_right = grand_slot(z_index)
    for step in range(1, depth):
        found = lax.ppermute(sent[step - 1], DEPTH, [(i, i ^ step) for i in range(depth)])
        grand_right = grand_right + found.astype(F32)
    grand_half_right = grand_right.astype(BF16)
    grand_right = pieces_along(grand_half_right, "h")

    late = [(after(piece, halves[0]), index) for piece, index in all_solved]

    def update_late(level, name):
        def product(start, count, dtype):
            value = times(
                panels, late, start, count, name=name, base=level * slice_rows,
                full=slice_rows, scale=row_mask[level], dtype=dtype,
            )
            return after(value, grand_half_right) if dtype == BF16 else value

        return split_product(product, slice_rows, "h")

    kept, arrived = update_late(1, "child_update")
    child_halves = [kept] + arrived
    kept, arrived = update_late(2, "root_update")
    root_half = total_of(kept, arrived)

    def to_depth(target):
        child_top = lax.dynamic_index_in_dim(top_part, 4 + target // 2, 0, keepdims=False)
        child_part = rows_at(
            child_top.astype(F32) - slot_sum(child_halves, 2 * (target // 2), 2),
            target % 2 * quarter,
            quarter,
        )
        root_part = rows_at(
            top_part[6].astype(F32) - root_half, target * share_rows, share_rows
        )
        return jnp.concatenate([child_part, root_part], axis=0)

    level_sum = to_depth(z_index)
    for step in range(1, depth):
        found = lax.ppermute(
            to_depth(z_index ^ step).astype(BF16), DEPTH, [(i, i ^ step) for i in range(depth)]
        )
        level_sum = level_sum + found.astype(F32)

    def placed(piece, start):
        blank = jnp.zeros((half_rows, side_count), F32)
        return lax.dynamic_update_slice_in_dim(blank, piece, start, 0)

    child_piece = placed(level_sum[:quarter], g_index * quarter)
    root_piece = placed(level_sum[quarter:], z_index * share_rows)

    def of(matrix, pieces, name, transposed=False, plus=None):
        def product(start, count, dtype):
            return times(
                matrix, pieces, start, count, name=name, transposed=transposed, plus=plus,
                dtype=dtype,
            )

        return product

    grand_rows = grand_inverse.shape[0]
    grand_solved = panel_solve(of(grand_lower, grand_right, "grand_solve"), grand_rows)

    kept, arrived = split_product(of(child_panels, grand_solved, "to_child"), slice_rows, "h")
    root_from_grand = of(root_grand, grand_solved, "grand_to_root")(lambda: 0, slice_rows, F32)
    child_own = child_piece - total_of(kept, arrived)
    child_right = total_of(child_own, others(child_own.astype(BF16), "g"))
    child_right = pieces_along(child_right.astype(BF16), "h")
    child_rows = child_inverse.shape[0]
    child_solved = panel_solve(of(child_lower, child_right, "child_solve"), child_rows)

    kept, arrived = split_product(
        of(root_child, child_solved, "to_root", plus=root_from_grand), slice_rows, "h"
    )
    root_own = root_piece - total_of(kept, arrived)
    root_right = total_of(root_own, depth_others(root_own.astype(BF16)))
    root_right = pieces_along(root_right.astype(BF16), "h")
    root_rows = root_inverse.shape[0]
    root_solved = panel_solve(of(root_lower, root_right, "root_solve"), root_rows)
    kept, arrived = split_product(
        of(root_lower, root_solved, "root_back", True), slice_rows, "h"
    )
    root_own = total_of(kept, arrived)
    root_half_result = total_of(root_own, depth_others(root_own.astype(BF16))).astype(BF16)
    root_result = pieces_along(root_half_result, "h")

    child_residual = panel_solve(
        of(root_child, root_result, "to_child_back", True), child_rows, child_solved
    )
    grand_back = of(root_grand, root_result, "root_to_grand", True)(lambda: 0, grand_rows, F32)
    whole_root = joined(root_result)
    pulled = times(
        panels, own(whole_root * row_mask[2]), lambda: 0, width, name="root_pull",
        transposed=True, base=2 * slice_rows,
    )
    kept, arrived = split_product(
        of(child_lower, child_residual, "child_back", True), slice_rows, "h"
    )
    child_own = total_of(kept, arrived)
    child_half = total_of(child_own, others(child_own.astype(BF16), "g")).astype(BF16)
    child_result = pieces_along(child_half, "h")

    grand_residual = panel_solve(
        of(child_panels, child_result, "to_grand_back", True, grand_back), grand_rows, grand_solved
    )
    whole_child = joined(child_result)
    other_child = shift(whole_child, "c", 1)
    kept, arrived = split_product(
        of(grand_lower, grand_residual, "grand_back", True), slice_rows, "h"
    )
    grand_half = total_of(kept, arrived).astype(BF16)

    grand_halves = [grand_half] + depth_others(grand_half)

    def grand_half_of(slot):
        found = grand_halves[0]
        for step in range(1, depth):
            found = jnp.where(slot == z_index ^ step, grand_halves[step], found)
        return found

    own_child = jnp.where(parent // 2 == lax.axis_index("c"), whole_child, other_child)
    pulled = times(
        panels, own(own_child * row_mask[1]), lambda: 0, width, name="child_pull",
        transposed=True, base=slice_rows, plus=pulled,
    )
    mine = [(grand_half_of(parent), hidx)]
    for step in range(1, owners):
        chosen = grand_half_of(parents[owners - step])
        mine.append(
            (shift(chosen, "h", step), lambda step=step: (lax.axis_index("h") - step) % owners)
        )
    own_grand = joined(mine) * row_mask[0]

    def panel_split(product, count):
        block = count // rows_y // 2
        size = rows_y

        def blocks_of(core, dtype):
            return [
                product(
                    lambda step=step: (
                        (lax.axis_index("y") + step) % size * 2 + (lax.axis_index("k") + core) % 2
                    ) * block,
                    block,
                    dtype,
                )
                for step in range(size)
            ]

        sent = [shift(value, "k", 1) for value in blocks_of(1, BF16)]
        held_blocks = blocks_of(0, F32)
        sums = [keep + found.astype(F32) for keep, found in zip(held_blocks, sent)]
        total = sums[0]
        for step in range(1, size):
            total = total + shift(sums[step].astype(BF16), "y", step).astype(F32)
        return total

    leaf_pulled = panel_split(
        lambda start, count, dtype: times(
            panels, own(own_grand), start, count, name="grand_pull", transposed=True,
            plus=pulled, dtype=dtype,
        ),
        width,
    )
    leaf_residual = (solved_leaf.astype(F32) - leaf_pulled).astype(BF16)
    leaf_solution = panel_split(
        of(leaf_lower, own(leaf_residual), "leaf_back", True), width
    ).astype(BF16)

    grand_block = jnp.zeros((4, share_rows, side_count), BF16)
    stacked = jnp.stack(
        [grand_half_of(jnp.int32(slot)) for slot in range(4)]
    )
    for step in range(owners):
        target = z_index * owners + (h_index + step) % owners
        block = lax.dynamic_slice_in_dim(stacked, target % depth * share_rows, share_rows, 1)
        if step:
            block = shift(after(block, own_grand), "h", step)
        holder = (h_index - step) % owners
        grand_block = jnp.where(leaf_index // depth == holder, block, grand_block)
    first_child = jnp.where(lax.axis_index("c") == 0, whole_child, other_child)
    second_child = jnp.where(lax.axis_index("c") == 0, other_child, whole_child)
    rest = [
        rows_at(value, leaf_index * share_rows, share_rows)[None]
        for value in (first_child, second_child, whole_root)
    ]
    return leaf_solution, jnp.concatenate([grand_block] + rest, axis=0)


def solution(mesh):
    leaf_count = mesh.shape["leaf"]
    panel_count = mesh.shape["panel"]
    split_mesh = Mesh(
        mesh.devices.reshape(2, 2, leaf_count // 4, panel_count // 2, 2), LEAF + PANEL
    )
    placed = (
        P(LEAF + PANEL, None),
        P(LEAF + PANEL, None),
        P(None, PANEL, LEAF),
        P(LEAF),
        P(LEAF, None, None),
        P(None, PANEL + LEAF, None),
        P(LEAF, PANEL),
        P(LEAF, PANEL),
        P(LEAF, PANEL),
        P(PANEL, LEAF),
        P(PANEL, LEAF),
        P(PANEL, LEAF),
    )
    return jax.shard_map(
        per_device,
        mesh=split_mesh,
        in_specs=placed,
        out_specs=(P(LEAF + PANEL, None), P(None, PANEL + LEAF, None)),
        check_vma=False,
    )
```

```python
import jax
import jax.numpy as jnp
from jax import lax
from jax.experimental import pallas as pl
from jax.experimental.pallas import tpu as pltpu
from jax.sharding import Mesh
from jax.sharding import PartitionSpec as P

TILE_ROWS = 128
LANES = 128
LEAF = ("c", "g", "h")
PANEL = ("y", "k")
DEPTH = ("c", "g")
F32 = jnp.float32
BF16 = jnp.bfloat16
VMEM = pltpu.VMEM


def held(value):
    return pltpu.with_memory_space_constraint(value, VMEM)


def after(value, other):
    return lax.optimization_barrier((value, other))[0]


def lower_part(matrix, row_offset, col_offset):
    row_index = row_offset + lax.broadcasted_iota(jnp.int32, matrix.shape, 0)
    col_index = col_offset + lax.broadcasted_iota(jnp.int32, matrix.shape, 1)
    return jnp.where(row_index >= col_index, matrix, jnp.zeros_like(matrix))


def rows_at(value, start, count):
    return lax.dynamic_slice_in_dim(value, start, count, 0)


def own(value):
    return [(value, lambda: 0)]


def joined(pieces):
    if len(pieces) == 1:
        return pieces[0][0]
    count = pieces[0][0].shape[0]
    place = lax.broadcasted_iota(jnp.int32, (len(pieces),) + pieces[0][0].shape, 0)
    whole = jnp.broadcast_to(pieces[0][0][None], place.shape)
    for value, index in pieces[1:]:
        whole = jnp.where(place == index(), value[None], whole)
    return whole.reshape((len(pieces) * count,) + pieces[0][0].shape[1:])


def block_of(pieces, wanted):
    found = pieces[0][0]
    for value, index in pieces[1:]:
        found = jnp.where(index() == wanted, value, found)
    return found


def loaded(matrices, level):
    rows, columns = matrices.shape[1:]
    parts = 4

    def kernel(from_ref, out_ref, sems):
        copies = []
        for part in range(parts):
            window = pl.ds(part * rows // parts, rows // parts)
            copy = pltpu.make_async_copy(
                from_ref.at[level, window], out_ref.at[window], sems.at[part]
            )
            copy.start()
            copies.append(copy)
        for copy in copies:
            copy.wait()

    return pl.pallas_call(
        kernel,
        out_shape=VMEM((rows, columns), matrices.dtype),
        in_specs=[pl.BlockSpec(memory_space=pltpu.HBM)],
        out_specs=pl.BlockSpec(memory_space=VMEM),
        scratch_shapes=[pltpu.SemaphoreType.DMA((parts,))],
        compiler_params=pltpu.CompilerParams(vmem_limit_bytes=1 << 20),
        cost_estimate=pl.CostEstimate(
            flops=0, bytes_accessed=2 * rows * columns, transcendentals=0
        ),
        name="load_panel",
    )(pltpu.with_memory_space_constraint(matrices, pltpu.HBM))


def times(
    matrix, pieces, starts, count, *, name, transposed=False, plus=None, minus=False,
    scale=None, mask=None, dtype=F32,
):
    if pieces[0][0].shape[0] % LANES:
        pieces = own(joined(pieces))
    full = matrix.shape[int(transposed)]
    if count % LANES and count < full:
        whole = times(
            matrix, pieces, [lambda: 0], full, name=name, transposed=transposed, plus=plus,
            minus=minus, scale=scale, mask=mask, dtype=dtype,
        )
        return jnp.concatenate([rows_at(whole, start(), count) for start in starts], axis=0)
    width = pieces[0][0].shape[0]
    sides = pieces[0][0].shape[1]
    extra = [value for value in (plus, scale, mask) if value is not None]

    def place(value):
        return pl.multiple_of(value, LANES)

    def kernel(matrix_ref, *refs):
        out_ref = refs[-1]
        vector_refs = refs[: len(pieces)]
        extra_refs = list(refs[len(pieces) : -1])
        plus_ref = extra_refs.pop(0) if plus is not None else None
        scale_ref = extra_refs.pop(0) if scale is not None else None
        mask_ref = extra_refs.pop(0) if mask is not None else None
        vectors = []
        for vector_ref, (_, index) in zip(vector_refs, pieces):
            rows = pl.ds(place(index() * width), width)
            vector = vector_ref[...]
            if mask is not None:
                vector = vector * mask_ref[rows, :]
            vectors.append((vector, rows))
        for step, start in enumerate(starts):
            window = pl.ds(place(start()) if count < full else 0, count)
            total = None
            for vector, rows in vectors:
                if transposed:
                    part = lax.dot_general(
                        vector,
                        matrix_ref[rows, window],
                        (((0,), (0,)), ((), ())),
                        preferred_element_type=F32,
                    )
                else:
                    part = jnp.dot(
                        matrix_ref[window, rows], vector, preferred_element_type=F32
                    )
                total = part if total is None else total + part
            if transposed:
                total = total.T
            if scale is not None:
                total = total * scale_ref[window, :].astype(F32)
            if plus is not None:
                before = plus_ref[window, :].astype(F32)
                total = before - total if minus else before + total
            out_ref[pl.ds(step * count, count), :] = total.astype(dtype)

    depth = len(pieces) * width
    return pl.pallas_call(
        kernel,
        out_shape=VMEM((len(starts) * count, sides), dtype),
        in_specs=[pl.BlockSpec(memory_space=VMEM)] * (1 + len(pieces) + len(extra)),
        out_specs=pl.BlockSpec(memory_space=VMEM),
        compiler_params=pltpu.CompilerParams(vmem_limit_bytes=6 << 20),
        cost_estimate=pl.CostEstimate(
            flops=2 * len(starts) * count * depth * sides,
            bytes_accessed=2 * len(starts) * count * depth,
            transcendentals=0,
        ),
        name=name,
    )(held(matrix), *[held(value) for value, _ in pieces], *[held(value) for value in extra])


def shift(value, axis, step):
    size = lax.axis_size(axis)
    return lax.ppermute(value, axis, [(i, (i + step) % size) for i in range(size)])


def others(value, axis):
    return [shift(value, axis, step) for step in range(1, lax.axis_size(axis))]


def pieces_along(value, axis):
    size = lax.axis_size(axis)
    found = [(value, lambda: lax.axis_index(axis))]
    for step in range(1, size):
        found.append(
            (shift(value, axis, step), lambda step=step: (lax.axis_index(axis) - step) % size)
        )
    return found


def split_product(product, count, axis):
    size = lax.axis_size(axis)
    block = count // size
    arrived = []
    for step in range(1, size):
        sent = product([lambda step=step: (lax.axis_index(axis) + step) % size * block], block, BF16)
        arrived.append(shift(sent, axis, step))
    kept = product([lambda: lax.axis_index(axis) * block], block, F32)
    return kept, arrived


def total_of(kept, arrived):
    for part in arrived:
        kept = kept + part.astype(F32)
    return kept


def panel_solve(product, count, less_from=None):
    half = total_of(*split_product(product, count, "k"))
    half = total_of(half, others(half.astype(BF16), "y"))
    if less_from is not None:
        half = less_from[0][0].astype(F32) - half
    return pieces_along(half.astype(BF16), "k")


def panel_split(product, count):
    rows_y = lax.axis_size("y")
    block = count // rows_y // 2

    def blocks_of(core, dtype):
        starts = [
            lambda step=step: (
                (lax.axis_index("y") + step) % rows_y * 2 + (lax.axis_index("k") + core) % 2
            ) * block
            for step in range(rows_y)
        ]
        return product(starts, block, dtype)

    sent = shift(blocks_of(1, BF16), "k", 1)
    sums = blocks_of(0, F32) + sent.astype(F32)
    total = sums[:block]
    for step in range(1, rows_y):
        moved = sums[step * block : (step + 1) * block].astype(BF16)
        total = total + shift(moved, "y", step).astype(F32)
    return total


def depth_others(value):
    size = lax.axis_size(DEPTH)
    return [
        lax.ppermute(value, DEPTH, [(i, i ^ step) for i in range(size)])
        for step in range(1, size)
    ]


def panel_pieces(value):
    found = []
    for piece, place_y in pieces_along(value, "y"):
        for item, place_k in pieces_along(piece, "k"):
            found.append((item, lambda a=place_y, b=place_k: a() * 2 + b()))
    return found


def per_device(
    leaf_sides,
    leaf_inverse,
    leaf_panels,
    parent_map,
    tile_mask,
    top_sides,
    grand_inverse,
    child_inverse,
    root_inverse,
    child_panels,
    root_grand,
    root_child,
):
    c_index = lax.axis_index("c")
    z_index = lax.axis_index(DEPTH)
    g_index = lax.axis_index("g")
    h_index = lax.axis_index("h")
    leaf_index = lax.axis_index(LEAF)
    panel_index = lax.axis_index(PANEL)
    owners = lax.axis_size("h")
    depth = lax.axis_size(DEPTH)
    part_rows = leaf_sides.shape[0]
    side_count = leaf_sides.shape[1]
    slice_rows = leaf_panels.shape[1]
    width = leaf_panels.shape[2]
    share_rows = top_sides.shape[1]
    half_rows = slice_rows // owners
    grand_rows = grand_inverse.shape[0]
    child_rows = child_inverse.shape[0]
    root_rows = root_inverse.shape[0]
    parent = parent_map[0]

    def of(matrix, pieces, name, **more):
        def product(starts, count, dtype):
            return times(matrix, pieces, starts, count, name=name, dtype=dtype, **more)

        return product

    sides = panel_pieces(leaf_sides)
    leaf_lower = held(lower_part(leaf_inverse, panel_index * part_rows, 0))
    panels = [loaded(leaf_panels, 0)]
    solved_leaf = times(leaf_lower, sides, [lambda: 0], part_rows, name="leaf_solve", dtype=BF16)
    all_solved = panel_pieces(solved_leaf)

    grand_lower = held(
        lower_part(
            after(grand_inverse, solved_leaf), h_index * grand_rows, panel_index * slice_rows
        )
    )
    tile_count = slice_rows // TILE_ROWS
    tile_rows = lax.dynamic_slice_in_dim(
        after(tile_mask, solved_leaf)[0], panel_index * tile_count, tile_count, 1
    )
    row_mask = [
        jnp.broadcast_to(
            tile_rows[level].astype(BF16)[:, None, None], (tile_count, TILE_ROWS, side_count)
        ).reshape(slice_rows, side_count)
        for level in range(3)
    ]

    note = jnp.broadcast_to(parent.astype(BF16), (16, side_count))
    packet = jnp.concatenate(
        [after(top_sides, solved_leaf).reshape(7 * share_rows, side_count), note], axis=0
    )
    packets = [(packet, parent, h_index)]
    for step in range(1, owners):
        found = shift(packet, "h", step)
        packets.append(
            (found, found[7 * share_rows, 0].astype(jnp.int32), (h_index - step) % owners)
        )
    parents = [item[1] for item in packets]
    place = lax.broadcasted_iota(jnp.int32, (7, depth, share_rows, side_count), 1)
    top_part = jnp.zeros(place.shape, BF16)
    for found, _, source in packets:
        holder = z_index * owners + source
        block = found[: 7 * share_rows].reshape(7, 1, share_rows, side_count)
        here = (place == holder % depth) & (holder // depth == h_index)
        top_part = jnp.where(here, block, top_part)
    top_part = top_part.reshape(7, half_rows, side_count)

    kept, arrived = split_product(
        of(panels[0], all_solved, "grand_update", scale=row_mask[0]), slice_rows, "h"
    )
    halves = [kept] + arrived

    def grand_slot(target):
        total = lax.dynamic_index_in_dim(top_part, target, 0, keepdims=False).astype(F32)
        for part, slot in zip(halves, parents):
            total = total - jnp.where(slot == target, part.astype(F32), 0.0)
        return total

    sent = [grand_slot(z_index ^ step).astype(BF16) for step in range(1, depth)]
    arrived = [
        lax.ppermute(sent[step - 1], DEPTH, [(i, i ^ step) for i in range(depth)])
        for step in range(1, depth)
    ]

    late_panels = after(leaf_panels, sent[0])
    panels += [loaded(late_panels, level) for level in (1, 2)]
    late = [(after(piece, sent[0]), index) for piece, index in all_solved]
    lower = [
        times(
            panels[level], late, [lambda: 0], slice_rows, name="lower_update",
            scale=row_mask[level],
        )
        for level in (1, 2)
    ]
    grand_half_right, lower[0], lower[1] = lax.optimization_barrier(
        (total_of(grand_slot(z_index), arrived).astype(BF16), lower[0], lower[1])
    )
    grand_right = pieces_along(grand_half_right, "h")

    def with_top(value, top):
        blank = jnp.zeros((slice_rows, side_count), F32)
        top_rows = lax.dynamic_update_slice_in_dim(
            blank, top.astype(F32), h_index * half_rows, 0
        )
        return top_rows - value

    def child_before(target):
        top = lax.dynamic_index_in_dim(top_part, 4 + target, 0, keepdims=False)
        return with_top(jnp.where(parent // 2 == target, lower[0], 0.0), top)

    child_before_own = child_before(c_index) + shift(
        child_before(1 - c_index).astype(BF16), "c", 1
    ).astype(F32)
    root_before = with_top(lower[1], top_part[6])

    root_pair = jnp.concatenate(
        [root_inverse, shift(after(root_inverse, sides[0][0]), "g", 1)], axis=0
    )
    root_far = shift(after(root_pair, grand_half_right), "c", 1)

    child_lower = held(
        lower_part(
            after(child_inverse, grand_half_right),
            (g_index * owners + h_index) * child_rows,
            panel_index * slice_rows,
        )
    )
    grand_solved = panel_solve(of(grand_lower, grand_right, "grand_solve"), grand_rows)

    kept, arrived = split_product(
        of(child_panels, grand_solved, "to_child", plus=child_before_own, minus=True),
        slice_rows,
        "h",
    )
    root_before = times(
        root_grand, grand_solved, [lambda: 0], slice_rows, name="grand_to_root",
        plus=root_before, minus=True,
    )
    child_own, root_before = lax.optimization_barrier((total_of(kept, arrived), root_before))
    child_right = total_of(child_own, others(child_own.astype(BF16), "g"))
    child_right = pieces_along(child_right.astype(BF16), "h")
    child_solved = panel_solve(of(child_lower, child_right, "child_solve"), child_rows)

    kept, arrived = split_product(
        of(root_child, child_solved, "to_root", plus=root_before, minus=True), slice_rows, "h"
    )
    root_all = jnp.concatenate([root_pair, root_far], axis=0)
    root_all = root_all.reshape(depth, root_rows, slice_rows)
    plane = z_index ^ lax.broadcasted_iota(jnp.int32, root_all.shape, 0)
    rows_of = (plane * owners + h_index) * root_rows
    rows_of = rows_of + lax.broadcasted_iota(jnp.int32, root_all.shape, 1)
    columns_of = panel_index * slice_rows + lax.broadcasted_iota(jnp.int32, root_all.shape, 2)
    root_lower = jnp.where(rows_of >= columns_of, root_all, jnp.zeros_like(root_all))
    root_lower = held(root_lower.reshape(depth * root_rows, slice_rows))
    root_own = total_of(kept, arrived)
    root_own = total_of(root_own, others(root_own.astype(BF16), "g"))
    root_own = total_of(root_own, others(root_own.astype(BF16), "c"))
    root_right = pieces_along(root_own.astype(BF16), "h")
    root_solved = panel_solve(of(root_lower, root_right, "root_solve"), depth * root_rows)
    root_part = times(
        root_lower, root_solved, [lambda: 0], slice_rows, name="root_back", transposed=True
    )
    root_result = own(total_of(root_part, others(root_part.astype(BF16), "h")).astype(BF16))

    child_residual = panel_solve(
        of(root_child, root_result, "to_child_back", transposed=True), child_rows, child_solved
    )
    grand_back = times(
        root_grand, root_result, [lambda: 0], grand_rows, name="root_to_grand", transposed=True
    )
    pulled = times(
        panels[2], root_result, [lambda: 0], width, name="root_pull", transposed=True,
        mask=row_mask[2],
    )
    residual, grand_back, pulled = lax.optimization_barrier(
        (child_residual[0][0], grand_back, pulled)
    )
    child_residual[0] = (residual, child_residual[0][1])
    child_own = total_of(
        *split_product(
            of(child_lower, child_residual, "child_back", transposed=True), slice_rows, "h"
        )
    )
    child_half = total_of(child_own, others(child_own.astype(BF16), "g")).astype(BF16)
    child_result = pieces_along(child_half, "h")

    grand_residual = panel_solve(
        of(child_panels, child_result, "to_grand_back", transposed=True, plus=grand_back),
        grand_rows,
        grand_solved,
    )
    child_stack = jnp.stack([value for value, _ in child_result])
    child_other = shift(child_stack, "c", 1)
    kept, arrived = split_product(
        of(grand_lower, grand_residual, "grand_back", transposed=True), slice_rows, "h"
    )
    grand_half = total_of(kept, arrived).astype(BF16)

    grand_halves = [grand_half] + depth_others(grand_half)

    def grand_half_of(slot):
        found = grand_halves[0]
        for step in range(1, depth):
            found = jnp.where(slot == z_index ^ step, grand_halves[step], found)
        return found

    child_chosen = jnp.where(parent // 2 == c_index, child_stack, after(child_other, grand_half))
    pulled = times(
        panels[1],
        [(child_chosen[step], index) for step, (_, index) in enumerate(child_result)],
        [lambda: 0],
        width,
        name="child_pull",
        transposed=True,
        mask=row_mask[1],
        plus=pulled,
    )
    mine, pulled = lax.optimization_barrier((grand_half_of(parent), pulled))
    grand_mine = [(mine, lambda: lax.axis_index("h"))]
    for step in range(1, owners):
        chosen = shift(grand_half_of(parents[owners - step]), "h", step)
        grand_mine.append((chosen, lambda step=step: (lax.axis_index("h") - step) % owners))

    leaf_pulled = panel_split(
        of(panels[0], grand_mine, "grand_pull", transposed=True, mask=row_mask[0], plus=pulled),
        width,
    )
    leaf_residual = (solved_leaf.astype(F32) - leaf_pulled).astype(BF16)
    leaf_solution = panel_split(
        of(leaf_lower, own(leaf_residual), "leaf_back", transposed=True), width
    ).astype(BF16)

    grand_block = jnp.zeros((4, share_rows, side_count), BF16)
    stacked = jnp.stack([grand_half_of(jnp.int32(slot)) for slot in range(4)])
    for step in range(owners):
        target = z_index * owners + (h_index + step) % owners
        block = lax.dynamic_slice_in_dim(stacked, target % depth * share_rows, share_rows, 1)
        if step:
            block = shift(after(block, grand_mine[-1][0]), "h", step)
        holder = (h_index - step) % owners
        grand_block = jnp.where(leaf_index // depth == holder, block, grand_block)
    holder = leaf_index // depth
    child_block = block_of(child_result, holder)
    other_block = block_of(
        [(child_other[step], index) for step, (_, index) in enumerate(child_result)], holder
    )
    first = jnp.where(c_index == 0, child_block, other_block)
    second = jnp.where(c_index == 0, other_block, child_block)
    offset = leaf_index % depth * share_rows
    rest = [
        rows_at(first, offset, share_rows)[None],
        rows_at(second, offset, share_rows)[None],
        rows_at(root_result[0][0], leaf_index * share_rows, share_rows)[None],
    ]
    return leaf_solution, jnp.concatenate([grand_block] + rest, axis=0)


def solution(mesh):
    leaf_count = mesh.shape["leaf"]
    panel_count = mesh.shape["panel"]
    split_mesh = Mesh(
        mesh.devices.reshape(2, 2, leaf_count // 4, panel_count // 2, 2), LEAF + PANEL
    )
    placed = (
        P(LEAF + PANEL, None),
        P(LEAF + PANEL, None),
        P(None, PANEL, LEAF),
        P(LEAF),
        P(LEAF, None, None),
        P(None, PANEL + LEAF, None),
        P(LEAF, PANEL),
        P(LEAF, PANEL),
        P(LEAF, PANEL),
        P(PANEL, LEAF),
        P(PANEL, LEAF),
        P(PANEL, LEAF),
    )
    return jax.shard_map(
        per_device,
        mesh=split_mesh,
        in_specs=placed,
        out_specs=(P(LEAF + PANEL, None), P(None, PANEL + LEAF, None)),
        check_vma=False,
    )
```

```python
import jax
import jax.numpy as jnp
from jax import lax
from jax.experimental import pallas as pl
from jax.experimental.pallas import tpu as pltpu
from jax.sharding import Mesh
from jax.sharding import PartitionSpec as P

TILE_ROWS = 128
LANES = 128
LEAF = ("c", "g", "h")
PANEL = ("y", "k")
DEPTH = ("c", "g")
F32 = jnp.float32
BF16 = jnp.bfloat16
VMEM = pltpu.VMEM


def after(value, other):
    return lax.optimization_barrier((value, other))[0]


def lower_part(matrix, row_offset, col_offset):
    row_index = row_offset + lax.broadcasted_iota(jnp.int32, matrix.shape, 0)
    col_index = col_offset + lax.broadcasted_iota(jnp.int32, matrix.shape, 1)
    return jnp.where(row_index >= col_index, matrix, jnp.zeros_like(matrix))


def rows_at(value, start, count, axis=0):
    starts = [jnp.int32(0)] * value.ndim
    starts[axis] = start
    sizes = list(value.shape)
    sizes[axis] = count
    return lax.dynamic_slice(value, starts, sizes, allow_negative_indices=False)


def row_at(value, index):
    return rows_at(value, index, 1)[0]


def own(value):
    return [(value, lambda: 0)]


def joined(pieces):
    if len(pieces) == 1:
        return pieces[0][0]
    count = pieces[0][0].shape[0]
    place = lax.broadcasted_iota(jnp.int32, (len(pieces),) + pieces[0][0].shape, 0)
    whole = jnp.broadcast_to(pieces[0][0][None], place.shape)
    for value, index in pieces[1:]:
        whole = jnp.where(place == index(), value[None], whole)
    return whole.reshape((len(pieces) * count,) + pieces[0][0].shape[1:])


def loaded(matrices, level):
    rows, columns = matrices.shape[1:]
    parts = 4

    def kernel(from_ref, out_ref, sems):
        copies = []
        for part in range(parts):
            window = pl.ds(part * (rows // parts), rows // parts)
            copy = pltpu.make_async_copy(
                from_ref.at[level, window], out_ref.at[window], sems.at[part]
            )
            copy.start()
            copies.append(copy)
        for copy in copies:
            copy.wait()

    return pl.pallas_call(
        kernel,
        out_shape=jax.ShapeDtypeStruct((rows, columns), matrices.dtype),
        in_specs=[pl.BlockSpec(memory_space=pltpu.HBM)],
        out_specs=pl.BlockSpec(memory_space=VMEM),
        scratch_shapes=[pltpu.SemaphoreType.DMA((parts,))],
        compiler_params=pltpu.CompilerParams(vmem_limit_bytes=5 << 20),
        cost_estimate=pl.CostEstimate(
            flops=0, bytes_accessed=2 * rows * columns, transcendentals=0
        ),
        name="load_panel",
    )(pltpu.with_memory_space_constraint(matrices, pltpu.HBM))


def lower_held(blocks, row_places, column_place):
    rows, columns = blocks[0].shape
    chunk = min(rows, 256)
    count = rows // chunk

    def kernel(*refs):
        out_ref, sems = refs[-2], refs[-1]
        copies = []
        for index in range(len(blocks)):
            for part in range(count):
                copy = pltpu.make_async_copy(
                    refs[index].at[pl.ds(part * chunk, chunk)],
                    out_ref.at[pl.ds((index * count + part) * chunk, chunk)],
                    sems.at[index * count + part],
                )
                copy.start()
                copies.append(copy)
        first_column = column_place()
        for index, row_place in enumerate(row_places):
            for part in range(count):
                copies[index * count + part].wait()
                window = pl.ds((index * count + part) * chunk, chunk)
                first_row = row_place() + part * chunk
                clear = first_row + chunk <= first_column

                @pl.when(clear)
                def _():
                    out_ref[window, :] = jnp.zeros((chunk, columns), BF16)

                @pl.when(jnp.logical_not(clear) & (first_row < first_column + columns - 1))
                def _():
                    out_ref[window, :] = lower_part(out_ref[window, :], first_row, first_column)

    return pl.pallas_call(
        kernel,
        out_shape=jax.ShapeDtypeStruct((len(blocks) * rows, columns), BF16),
        in_specs=[pl.BlockSpec(memory_space=pltpu.HBM)] * len(blocks),
        out_specs=pl.BlockSpec(memory_space=VMEM),
        scratch_shapes=[pltpu.SemaphoreType.DMA((len(blocks) * count,))],
        compiler_params=pltpu.CompilerParams(vmem_limit_bytes=4 << 20),
        cost_estimate=pl.CostEstimate(
            flops=0, bytes_accessed=2 * len(blocks) * rows * columns, transcendentals=0
        ),
        name="lower_held",
    )(*[pltpu.with_memory_space_constraint(block, pltpu.HBM) for block in blocks])


def times(
    matrix, pieces, starts, count, *, name, transposed=False, plus=None, minus=False,
    tiles=None, dtype=F32,
):
    if pieces[0][0].shape[0] % LANES:
        pieces = own(joined(pieces))
    full = matrix.shape[int(transposed)]
    if count % LANES and count < full:
        whole = times(
            matrix, pieces, [lambda: 0], full, name=name, transposed=transposed, plus=plus,
            minus=minus, tiles=tiles, dtype=dtype,
        )
        return jnp.concatenate([rows_at(whole, start(), count) for start in starts], axis=0)
    width = pieces[0][0].shape[0]
    sides = pieces[0][0].shape[1]
    extra = [] if plus is None else [plus]
    flags = [] if tiles is None else [tiles[0]]

    def place(value):
        return pl.multiple_of(value, LANES)

    def kernel(matrix_ref, *refs):
        out_ref = refs[-1]
        vector_refs = refs[: len(pieces)]
        plus_ref = refs[len(pieces)]
        flag_ref = refs[-2]

        def masked(value, first):
            tile = lax.axis_index(PANEL) * (panel_rows // TILE_ROWS) + first // TILE_ROWS
            parts = [
                value[part * TILE_ROWS : (part + 1) * TILE_ROWS]
                * flag_ref[0, tiles[1], tile + part].astype(F32).astype(value.dtype)
                for part in range(value.shape[0] // TILE_ROWS)
            ]
            return jnp.concatenate(parts, axis=0)

        vectors = []
        for vector_ref, (_, index) in zip(vector_refs, pieces):
            first = place(index() * width)
            vector = vector_ref[...]
            if tiles is not None and transposed:
                vector = masked(vector, first)
            vectors.append((vector, pl.ds(first, width)))
        for step, start in enumerate(starts):
            first = place(start()) if count < full else 0
            window = pl.ds(first, count)
            total = None
            for vector, rows in vectors:
                if transposed:
                    part = lax.dot_general(
                        vector,
                        matrix_ref[rows, window],
                        (((0,), (0,)), ((), ())),
                        preferred_element_type=F32,
                    )
                else:
                    part = jnp.dot(
                        matrix_ref[window, rows], vector, preferred_element_type=F32
                    )
                total = part if total is None else total + part
            if transposed:
                total = total.T
            if tiles is not None and not transposed:
                total = masked(total, first)
            if plus is not None:
                before = plus_ref[window, :].astype(F32)
                total = before - total if minus else before + total
            out_ref[pl.ds(step * count, count), :] = total.astype(dtype)

    depth = len(pieces) * width
    panel_rows = matrix.shape[0]
    return pl.pallas_call(
        kernel,
        out_shape=jax.ShapeDtypeStruct((len(starts) * count, sides), dtype),
        in_specs=[pl.BlockSpec(memory_space=VMEM)] * (1 + len(pieces) + len(extra))
        + [pl.BlockSpec(memory_space=pltpu.SMEM)] * len(flags),
        out_specs=pl.BlockSpec(memory_space=VMEM),
        compiler_params=pltpu.CompilerParams(vmem_limit_bytes=8 << 20),
        cost_estimate=pl.CostEstimate(
            flops=2 * len(starts) * count * depth * sides,
            bytes_accessed=2 * len(starts) * count * depth,
            transcendentals=0,
        ),
        name=name,
    )(matrix, *[value for value, _ in pieces], *extra, *flags)


def glue(kernel, outs, vectors, parents, name):
    return pl.pallas_call(
        kernel,
        out_shape=[jax.ShapeDtypeStruct(shape, dtype) for shape, dtype in outs],
        in_specs=[pl.BlockSpec(memory_space=VMEM)] * len(vectors)
        + [pl.BlockSpec(memory_space=pltpu.SMEM)],
        out_specs=[pl.BlockSpec(memory_space=VMEM)] * len(outs),
        compiler_params=pltpu.CompilerParams(vmem_limit_bytes=6 << 20),
        cost_estimate=pl.CostEstimate(
            flops=0, bytes_accessed=sum(2 * value.size for value in vectors), transcendentals=0
        ),
        name=name,
    )(*vectors, parents)


def shift(value, axis, step):
    size = lax.axis_size(axis)
    return lax.ppermute(value, axis, [(i, (i + step) % size) for i in range(size)])


def others(value, axis):
    return [shift(value, axis, step) for step in range(1, lax.axis_size(axis))]


def pieces_along(value, axis):
    size = lax.axis_size(axis)
    found = [(value, lambda: lax.axis_index(axis))]
    for step in range(1, size):
        found.append(
            (shift(value, axis, step), lambda step=step: (lax.axis_index(axis) - step) % size)
        )
    return found


def split_product(product, count, axis):
    size = lax.axis_size(axis)
    block = count // size
    arrived = []
    for step in range(1, size):
        sent = product([lambda step=step: (lax.axis_index(axis) + step) % size * block], block, BF16)
        arrived.append(shift(sent, axis, step))
    kept = product([lambda: lax.axis_index(axis) * block], block, F32)
    return kept, arrived


def total_of(kept, arrived):
    for part in arrived:
        kept = kept + part.astype(F32)
    return kept


def panel_solve(product, count, less_from=None):
    half = total_of(*split_product(product, count, "k"))
    half = total_of(half, others(half.astype(BF16), "y"))
    if less_from is not None:
        half = less_from[0][0].astype(F32) - half
    return pieces_along(half.astype(BF16), "k")


def panel_split(product, count):
    rows_y = lax.axis_size("y")
    block = count // rows_y // 2

    def blocks_of(core, dtype):
        starts = [
            lambda step=step: (
                (lax.axis_index("y") + step) % rows_y * 2 + (lax.axis_index("k") + core) % 2
            ) * block
            for step in range(rows_y)
        ]
        return product(starts, block, dtype)

    sent = shift(blocks_of(1, BF16), "k", 1)
    sums = blocks_of(0, F32) + sent.astype(F32)
    total = sums[:block]
    for step in range(1, rows_y):
        moved = sums[step * block : (step + 1) * block].astype(BF16)
        total = total + shift(moved, "y", step).astype(F32)
    return total


def depth_others(value):
    size = lax.axis_size(DEPTH)
    return [
        lax.ppermute(value, DEPTH, [(i, i ^ step) for i in range(size)])
        for step in range(1, size)
    ]


def panel_pieces(value):
    found = []
    for piece, place_y in pieces_along(value, "y"):
        for item, place_k in pieces_along(piece, "k"):
            found.append((item, lambda a=place_y, b=place_k: a() * 2 + b()))
    return found


def per_device(
    leaf_sides,
    leaf_inverse,
    leaf_panels,
    parent_map,
    tile_mask,
    top_sides,
    grand_inverse,
    child_inverse,
    root_inverse,
    child_panels,
    root_grand,
    root_child,
):
    owners = lax.axis_size("h")
    depth = lax.axis_size(DEPTH)
    part_rows = leaf_sides.shape[0]
    side_count = leaf_sides.shape[1]
    slice_rows = leaf_panels.shape[1]
    width = leaf_panels.shape[2]
    share_rows = top_sides.shape[1]
    half_rows = slice_rows // owners
    grand_rows = grand_inverse.shape[0]
    child_rows = child_inverse.shape[0]
    root_rows = root_inverse.shape[0]

    def of(matrix, pieces, name, **more):
        def product(starts, count, dtype):
            return times(matrix, pieces, starts, count, name=name, dtype=dtype, **more)

        return product

    parents = jnp.concatenate([parent_map] + others(parent_map, "h"))
    sides = panel_pieces(leaf_sides)
    last, parents = lax.optimization_barrier((sides[-1][0], parents))
    sides[-1] = (last, sides[-1][1])

    def add_top(out_ref, slot, packet_refs, base):
        for step, packet_ref in enumerate(packet_refs):
            source = lax.axis_index(DEPTH) * owners + (lax.axis_index("h") - step) % owners

            @pl.when(source // depth == lax.axis_index("h"))
            def _():
                first = pl.multiple_of(base + source % depth * share_rows, share_rows)
                rows = pl.ds(first, share_rows)
                total = out_ref[rows, :].astype(F32) + packet_ref[slot].astype(F32)
                out_ref[rows, :] = total.astype(out_ref.dtype)

    leaf_lower = lower_held([leaf_inverse], [lambda: lax.axis_index(PANEL) * part_rows], lambda: 0)
    panels = [loaded(leaf_panels, 0)]
    solved_leaf = times(leaf_lower, sides, [lambda: 0], part_rows, name="leaf_solve", dtype=BF16)
    all_solved = panel_pieces(solved_leaf)

    def panel_column():
        return lax.axis_index(PANEL) * slice_rows

    grand_lower = lower_held(
        [after(grand_inverse, solved_leaf)], [lambda: lax.axis_index("h") * grand_rows], panel_column
    )
    packet = after(top_sides, solved_leaf)
    packets = [packet] + others(packet, "h")
    kept, arrived = split_product(
        of(panels[0], all_solved, "grand_update", tiles=(tile_mask, 0)), slice_rows, "h"
    )
    def slots_kernel(*refs):
        half_refs, packet_refs = refs[:owners], refs[owners : 2 * owners]
        parent_ref, out_refs = refs[2 * owners], refs[2 * owners + 1 :]
        for step, out_ref in enumerate(out_refs):
            slot = lax.axis_index(DEPTH) ^ step
            total = jnp.zeros((half_rows, side_count), F32)
            for index, half_ref in enumerate(half_refs):
                chosen = (parent_ref[index] == slot).astype(F32)
                total = total - half_ref[...].astype(F32) * chosen
            out_ref[...] = total.astype(out_ref.dtype)
            add_top(out_ref, slot, packet_refs, 0)

    half_shape = (half_rows, side_count)
    slots = glue(
        slots_kernel,
        [(half_shape, F32)] + [(half_shape, BF16)] * (depth - 1),
        [kept] + arrived + packets,
        parents,
        "grand_slots",
    )
    sent = slots[1:]
    arrived = [
        lax.ppermute(sent[step - 1], DEPTH, [(i, i ^ step) for i in range(depth)])
        for step in range(1, depth)
    ]

    late = [(after(piece, sent[0]), index) for piece, index in all_solved]
    panels += [loaded(after(leaf_panels, sent[0]), level) for level in (1, 2)]
    lower = [
        times(
            panels[level], late, [lambda: 0], slice_rows, name="lower_update",
            tiles=(tile_mask, level),
        )
        for level in (1, 2)
    ]
    grand_half_right, lower[0], lower[1] = lax.optimization_barrier(
        (total_of(slots[0], arrived).astype(BF16), lower[0], lower[1])
    )
    grand_right = pieces_along(grand_half_right, "h")

    def before_kernel(*refs):
        lower_refs, packet_refs = refs[:2], refs[2 : 2 + owners]
        parent_ref, out_refs = refs[2 + owners], refs[3 + owners :]
        mine = (parent_ref[0] // 2 == lax.axis_index("c")).astype(F32)
        base = lax.axis_index("h") * half_rows
        tops = (4 + lax.axis_index("c"), 5 - lax.axis_index("c"), 6)
        for level, weight, top, out_ref in zip((0, 0, 1), (mine, 1.0 - mine, 1.0), tops, out_refs):
            out_ref[...] = (lower_refs[level][...] * -weight).astype(out_ref.dtype)
            add_top(out_ref, top, packet_refs, base)

    slice_shape = (slice_rows, side_count)
    child_before, child_before_other, root_before = glue(
        before_kernel,
        [(slice_shape, F32), (slice_shape, BF16), (slice_shape, F32)],
        lower + packets,
        parents,
        "lower_before",
    )
    child_before_own = child_before + shift(child_before_other, "c", 1).astype(F32)

    child_lower = lower_held(
        [after(child_inverse, grand_half_right)],
        [lambda: (lax.axis_index("g") * owners + lax.axis_index("h")) * child_rows],
        panel_column,
    )
    root_near = shift(after(root_inverse, solved_leaf), "g", 1)

    def root_place(step):
        plane = lax.axis_index("c") * 2 + (lax.axis_index("g") + step) % 2
        return (plane * owners + lax.axis_index("h")) * root_rows

    grand_solved = panel_solve(of(grand_lower, grand_right, "grand_solve"), grand_rows)

    kept, arrived = split_product(
        of(child_panels, grand_solved, "to_child", plus=child_before_own, minus=True),
        slice_rows,
        "h",
    )
    root_before = times(
        root_grand, grand_solved, [lambda: 0], slice_rows, name="grand_to_root",
        plus=root_before, minus=True,
    )
    child_own, root_before = lax.optimization_barrier((total_of(kept, arrived), root_before))
    child_right = total_of(child_own, others(child_own.astype(BF16), "g"))
    child_right = pieces_along(child_right.astype(BF16), "h")
    child_solved = panel_solve(of(child_lower, child_right, "child_solve"), child_rows)

    kept, arrived = split_product(
        of(root_child, child_solved, "to_root", plus=root_before, minus=True), slice_rows, "h"
    )
    root_lower = lower_held(
        [after(root_inverse, child_right[0][0]), root_near],
        [lambda: root_place(0), lambda: root_place(1)],
        panel_column,
    )
    root_own = total_of(kept, arrived)
    root_own = total_of(root_own, others(root_own.astype(BF16), "g"))
    root_own = total_of(root_own, others(root_own.astype(BF16), "c"))
    root_right = pieces_along(root_own.astype(BF16), "h")
    root_solved = panel_solve(of(root_lower, root_right, "root_solve"), 2 * root_rows)
    root_own = total_of(
        *split_product(
            of(root_lower, root_solved, "root_back", transposed=True), slice_rows, "h"
        )
    )
    root_half = total_of(root_own, others(root_own.astype(BF16), "c")).astype(BF16)
    root_result = pieces_along(root_half, "h")

    child_residual = panel_solve(
        of(root_child, root_result, "to_child_back", transposed=True), child_rows, child_solved
    )
    grand_back = times(
        root_grand, root_result, [lambda: 0], grand_rows, name="root_to_grand", transposed=True
    )
    pulled = times(
        panels[2], root_result, [lambda: 0], width, name="root_pull", transposed=True,
        tiles=(tile_mask, 2),
    )
    residual, grand_back, pulled = lax.optimization_barrier(
        (child_residual[0][0], grand_back, pulled)
    )
    child_residual[0] = (residual, child_residual[0][1])
    child_own = total_of(
        *split_product(
            of(child_lower, child_residual, "child_back", transposed=True), slice_rows, "h"
        )
    )
    child_half = total_of(child_own, others(child_own.astype(BF16), "g")).astype(BF16)
    child_result = pieces_along(child_half, "h")

    grand_residual = panel_solve(
        of(child_panels, child_result, "to_grand_back", transposed=True, plus=grand_back),
        grand_rows,
        grand_solved,
    )
    child_stack = jnp.stack([value for value, _ in child_result])
    child_other = shift(child_stack, "c", 1)
    kept, arrived = split_product(
        of(grand_lower, grand_residual, "grand_back", transposed=True), slice_rows, "h"
    )
    grand_half = total_of(kept, arrived).astype(BF16)

    grand_halves = [grand_half] + depth_others(grand_half)

    def chosen_kernel(own_ref, other_ref, parent_ref, out_ref):
        mine = parent_ref[0] // 2 == lax.axis_index("c")

        @pl.when(mine)
        def _():
            out_ref[...] = own_ref[...]

        @pl.when(jnp.logical_not(mine))
        def _():
            out_ref[...] = other_ref[...]

    child_chosen = glue(
        chosen_kernel,
        [(child_stack.shape, BF16)],
        [child_stack, after(child_other, grand_half)],
        parents,
        "child_chosen",
    )[0]
    pulled = times(
        panels[1],
        [(child_chosen[step], index) for step, (_, index) in enumerate(child_result)],
        [lambda: 0],
        width,
        name="child_pull",
        transposed=True,
        tiles=(tile_mask, 1),
        plus=pulled,
    )

    def results_kernel(*refs):
        half_refs, parent_ref = refs[:depth], refs[depth]
        mine_refs = refs[depth + 1 : depth + 1 + owners]
        block_refs = refs[depth + 1 + owners :]
        for step in range(depth):
            slot = lax.axis_index(DEPTH) ^ step
            for index in range(owners):

                @pl.when(parent_ref[(owners - index) % owners] == slot)
                def _():
                    mine_refs[index][...] = half_refs[step][...]

                target = lax.axis_index(DEPTH) * owners + (lax.axis_index("h") + index) % owners
                first = pl.multiple_of(target % depth * share_rows, share_rows)
                block_refs[index][slot] = half_refs[step][pl.ds(first, share_rows), :]

    block_shape = (depth, share_rows, side_count)
    results = glue(
        results_kernel,
        [(half_shape, BF16)] * owners + [(block_shape, BF16)] * owners,
        grand_halves,
        parents,
        "grand_results",
    )
    blocks = results[owners:]
    mine, pulled = lax.optimization_barrier((results[0], pulled))
    grand_mine = [(mine, lambda: lax.axis_index("h"))]
    for step in range(1, owners):
        grand_mine.append(
            (
                shift(results[step], "h", step),
                lambda step=step: (lax.axis_index("h") - step) % owners,
            )
        )

    leaf_pulled = panel_split(
        of(panels[0], grand_mine, "grand_pull", transposed=True, tiles=(tile_mask, 0), plus=pulled),
        width,
    )
    leaf_residual = (solved_leaf.astype(F32) - leaf_pulled).astype(BF16)
    leaf_solution = panel_split(
        of(leaf_lower, own(leaf_residual), "leaf_back", transposed=True), width
    ).astype(BF16)

    arrived = [blocks[0]] + [
        shift(after(blocks[step], grand_mine[-1][0]), "h", step) for step in range(1, owners)
    ]

    def tops_kernel(*refs):
        block_refs, root_refs = refs[:owners], refs[owners : 2 * owners]
        child_refs = refs[2 * owners : 2 * owners + 2]
        out_ref = refs[-1]
        holder = lax.axis_index(LEAF) // depth
        rows = pl.ds(
            pl.multiple_of(lax.axis_index(LEAF) % depth * share_rows, share_rows), share_rows
        )
        for step in range(owners):

            @pl.when((lax.axis_index("h") - step) % owners == holder)
            def _():
                out_ref[0:depth] = block_refs[step][...]
                out_ref[4 + lax.axis_index("c")] = child_refs[0][step, rows, :]
                out_ref[5 - lax.axis_index("c")] = child_refs[1][step, rows, :]
                out_ref[6] = root_refs[step][rows, :]

    top_solution = glue(
        tops_kernel,
        [((7, share_rows, side_count), BF16)],
        arrived + [value for value, _ in root_result] + [child_stack, child_other],
        parents,
        "top_results",
    )[0]
    return leaf_solution, top_solution


def solution(mesh):
    leaf_count = mesh.shape["leaf"]
    panel_count = mesh.shape["panel"]
    split_mesh = Mesh(
        mesh.devices.reshape(2, 2, leaf_count // 4, panel_count // 2, 2), LEAF + PANEL
    )
    placed = (
        P(LEAF + PANEL, None),
        P(LEAF + PANEL, None),
        P(None, PANEL, LEAF),
        P(LEAF),
        P(LEAF, None, None),
        P(None, PANEL + LEAF, None),
        P(LEAF, PANEL),
        P(LEAF, PANEL),
        P(LEAF, PANEL),
        P(PANEL, LEAF),
        P(PANEL, LEAF),
        P(PANEL, LEAF),
    )
    return jax.shard_map(
        per_device,
        mesh=split_mesh,
        in_specs=placed,
        out_specs=(P(LEAF + PANEL, None), P(None, PANEL + LEAF, None)),
        check_vma=False,
    )
```

```python
import jax
import jax.numpy as jnp
from jax import lax
from jax.experimental import pallas as pl
from jax.experimental.pallas import tpu as pltpu
from jax.sharding import Mesh
from jax.sharding import PartitionSpec as P


TILE_ROWS = 128
LANES = 128
LEAF = ("c", "g", "h")
PANEL = ("y", "k")
DEPTH = ("c", "g")
F32 = jnp.float32
BF16 = jnp.bfloat16
VMEM = pltpu.VMEM


def after(value, other):
    return lax.optimization_barrier((value, other))[0]


def lower_part(matrix, row_offset, col_offset):
    row_index = row_offset + lax.broadcasted_iota(jnp.int32, matrix.shape, 0)
    col_index = col_offset + lax.broadcasted_iota(jnp.int32, matrix.shape, 1)
    return jnp.where(row_index >= col_index, matrix, jnp.zeros_like(matrix))


def rows_at(value, start, count, axis=0):
    starts = [jnp.int32(0)] * value.ndim
    starts[axis] = start
    sizes = list(value.shape)
    sizes[axis] = count
    return lax.dynamic_slice(value, starts, sizes, allow_negative_indices=False)


def own(value):
    return [(value, lambda: 0)]


def joined(pieces):
    if len(pieces) == 1:
        return pieces[0][0]
    count = pieces[0][0].shape[0]
    place = lax.broadcasted_iota(jnp.int32, (len(pieces),) + pieces[0][0].shape, 0)
    whole = jnp.broadcast_to(pieces[0][0][None], place.shape)
    for value, index in pieces[1:]:
        whole = jnp.where(place == index(), value[None], whole)
    return whole.reshape((len(pieces) * count,) + pieces[0][0].shape[1:])


def loaded(matrices, level):
    rows, columns = matrices.shape[1:]
    parts = 4

    def kernel(from_ref, out_ref, sems):
        copies = []
        for part in range(parts):
            window = pl.ds(part * (rows // parts), rows // parts)
            copy = pltpu.make_async_copy(
                from_ref.at[level, window], out_ref.at[window], sems.at[part]
            )
            copy.start()
            copies.append(copy)
        for copy in copies:
            copy.wait()

    return pl.pallas_call(
        kernel,
        out_shape=jax.ShapeDtypeStruct((rows, columns), matrices.dtype),
        in_specs=[pl.BlockSpec(memory_space=pltpu.HBM)],
        out_specs=pl.BlockSpec(memory_space=VMEM),
        scratch_shapes=[pltpu.SemaphoreType.DMA((parts,))],
        compiler_params=pltpu.CompilerParams(vmem_limit_bytes=5 << 20),
        cost_estimate=pl.CostEstimate(
            flops=0, bytes_accessed=2 * rows * columns, transcendentals=0
        ),
        name="lp",
    )(pltpu.with_memory_space_constraint(matrices, pltpu.HBM))


def spread_flags(tile_mask, rows, sides):
    def kernel(flag_ref, out_ref):
        tile = lax.axis_index(PANEL) * (rows // TILE_ROWS)
        for level in range(3):
            for part in range(rows // TILE_ROWS):
                flag = flag_ref[0, level, tile + part].astype(F32)
                out_ref[level, part * TILE_ROWS : (part + 1) * TILE_ROWS, :] = jnp.full(
                    (TILE_ROWS, sides), flag, F32
                ).astype(BF16)

    return pl.pallas_call(
        kernel,
        out_shape=jax.ShapeDtypeStruct((3, rows, sides), BF16),
        in_specs=[pl.BlockSpec(memory_space=pltpu.SMEM)],
        out_specs=pl.BlockSpec(memory_space=VMEM),
        compiler_params=pltpu.CompilerParams(vmem_limit_bytes=2 << 20),
        name="fl",
    )(tile_mask)


def lower_held(blocks, row_places, column_place):
    rows, columns = blocks[0].shape
    chunk = min(rows, 256)
    count = rows // chunk

    def kernel(*refs):
        out_ref, sems = refs[-2], refs[-1]
        copies = []
        for index in range(len(blocks)):
            for part in range(count):
                copy = pltpu.make_async_copy(
                    refs[index].at[pl.ds(part * chunk, chunk)],
                    out_ref.at[pl.ds((index * count + part) * chunk, chunk)],
                    sems.at[index * count + part],
                )
                copy.start()
                copies.append(copy)
        first_column = column_place()
        for index, row_place in enumerate(row_places):
            for part in range(count):
                copies[index * count + part].wait()
                window = pl.ds((index * count + part) * chunk, chunk)
                first_row = row_place() + part * chunk
                clear = first_row + chunk <= first_column

                @pl.when(clear)
                def _():
                    out_ref[window, :] = jnp.zeros((chunk, columns), BF16)

                @pl.when(jnp.logical_not(clear) & (first_row < first_column + columns - 1))
                def _():
                    out_ref[window, :] = lower_part(out_ref[window, :], first_row, first_column)

    return pl.pallas_call(
        kernel,
        out_shape=jax.ShapeDtypeStruct((len(blocks) * rows, columns), BF16),
        in_specs=[pl.BlockSpec(memory_space=pltpu.HBM)] * len(blocks),
        out_specs=pl.BlockSpec(memory_space=VMEM),
        scratch_shapes=[pltpu.SemaphoreType.DMA((len(blocks) * count,))],
        compiler_params=pltpu.CompilerParams(vmem_limit_bytes=4 << 20),
        cost_estimate=pl.CostEstimate(
            flops=0, bytes_accessed=2 * len(blocks) * rows * columns, transcendentals=0
        ),
    )(*[pltpu.with_memory_space_constraint(block, pltpu.HBM) for block in blocks])


def times(
    matrix, pieces, starts, count, *, name, transposed=False, plus=None, minus=False,
    tiles=None, dtype=F32,
):
    if pieces[0][0].shape[0] % LANES:
        pieces = own(joined(pieces))
    full = matrix.shape[int(transposed)]
    if count % LANES and count < full:
        whole = times(
            matrix, pieces, [lambda: 0], full, name=name, transposed=transposed, plus=plus,
            minus=minus, tiles=tiles, dtype=dtype,
        )
        return jnp.concatenate([rows_at(whole, start(), count) for start in starts], axis=0)
    width = pieces[0][0].shape[0]
    sides = pieces[0][0].shape[1]
    extra = [] if plus is None else [plus]
    flags = [] if tiles is None else [tiles[0]]

    def place(value):
        return pl.multiple_of(value, LANES)

    def kernel(matrix_ref, *refs):
        out_ref = refs[-1]
        vector_refs = refs[: len(pieces)]
        plus_ref = refs[len(pieces)]
        flag_ref = refs[-2]

        vectors = []
        for vector_ref, (_, index) in zip(vector_refs, pieces):
            first = place(index() * width)
            vector = vector_ref[...]
            if tiles is not None and transposed:
                vector = vector * flag_ref[tiles[1], pl.ds(first, width), :]
            vectors.append((vector, pl.ds(first, width)))
        for step, start in enumerate(starts):
            first = place(start()) if count < full else 0
            window = pl.ds(first, count)
            total = None
            for vector, rows in vectors:
                if transposed:
                    part = lax.dot_general(
                        vector,
                        matrix_ref[rows, window],
                        (((0,), (0,)), ((), ())),
                        preferred_element_type=F32,
                    )
                else:
                    part = jnp.dot(
                        matrix_ref[window, rows], vector, preferred_element_type=F32
                    )
                total = part if total is None else total + part
            if transposed:
                total = total.T
            if tiles is not None and not transposed:
                total = total * flag_ref[tiles[1], window, :].astype(F32)
            if plus is not None:
                before = plus_ref[window, :].astype(F32)
                total = before - total if minus else before + total
            out_ref[pl.ds(step * count, count), :] = total.astype(dtype)

    depth = len(pieces) * width
    return pl.pallas_call(
        kernel,
        out_shape=jax.ShapeDtypeStruct((len(starts) * count, sides), dtype),
        in_specs=[pl.BlockSpec(memory_space=VMEM)] * (1 + len(pieces) + len(extra) + len(flags)),
        out_specs=pl.BlockSpec(memory_space=VMEM),
        compiler_params=pltpu.CompilerParams(vmem_limit_bytes=8 << 20),
        cost_estimate=pl.CostEstimate(
            flops=2 * len(starts) * count * depth * sides,
            bytes_accessed=2 * len(starts) * count * depth,
            transcendentals=0,
        ),
    )(matrix, *[value for value, _ in pieces], *extra, *flags)


def glue(kernel, outs, vectors, parents):
    return pl.pallas_call(
        kernel,
        out_shape=[jax.ShapeDtypeStruct(shape, dtype) for shape, dtype in outs],
        in_specs=[pl.BlockSpec(memory_space=VMEM)] * len(vectors)
        + [pl.BlockSpec(memory_space=pltpu.SMEM)] * len(parents),
        out_specs=[pl.BlockSpec(memory_space=VMEM)] * len(outs),
        compiler_params=pltpu.CompilerParams(vmem_limit_bytes=6 << 20),
        cost_estimate=pl.CostEstimate(
            flops=0, bytes_accessed=sum(2 * value.size for value in vectors), transcendentals=0
        ),
    )(*vectors, *parents)


def shift(value, axis, step):
    size = lax.axis_size(axis)
    return lax.ppermute(value, axis, [(i, (i + step) % size) for i in range(size)])


def others(value, axis):
    return [shift(value, axis, step) for step in range(1, lax.axis_size(axis))]


def pieces_along(value, axis):
    size = lax.axis_size(axis)
    found = [(value, lambda: lax.axis_index(axis))]
    for step in range(1, size):
        found.append(
            (
                shift(value, axis, step),
                lambda step=step: (lax.axis_index(axis) - step) % size,
            )
        )
    return found


def split_product(product, count, axis):
    size = lax.axis_size(axis)
    block = count // size
    arrived = []
    for step in range(1, size):
        sent = product([lambda step=step: (lax.axis_index(axis) + step) % size * block], block, BF16)
        arrived.append(shift(sent, axis, step))
    kept = product([lambda: lax.axis_index(axis) * block], block, F32)
    return kept, arrived


def total_of(kept, arrived):
    for part in arrived:
        kept = kept + part.astype(F32)
    return kept


def panel_solve(product, count, less_from=None):
    half = total_of(*split_product(product, count, "k"))
    half = total_of(half, others(half.astype(BF16), "y"))
    if less_from is not None:
        half = less_from[0][0].astype(F32) - half
    return pieces_along(half.astype(BF16), "k")


def panel_split(product, count):
    rows_y = lax.axis_size("y")
    block = count // rows_y // 2

    def blocks_of(core, dtype):
        starts = [
            lambda step=step: (
                (lax.axis_index("y") + step) % rows_y * 2 + (lax.axis_index("k") + core) % 2
            ) * block
            for step in range(rows_y)
        ]
        return product(starts, block, dtype)

    sent = shift(blocks_of(1, BF16), "k", 1)
    sums = blocks_of(0, F32) + sent.astype(F32)
    total = sums[:block]
    for step in range(1, rows_y):
        moved = sums[step * block : (step + 1) * block].astype(BF16)
        total = total + shift(moved, "y", step).astype(F32)
    return total


def depth_shift(value, step):
    size = lax.axis_size(DEPTH)
    return lax.ppermute(value, DEPTH, [(i, i ^ step) for i in range(size)])


def panel_pieces(value):
    found = []
    for piece, place_y in pieces_along(value, "y"):
        for item, place_k in pieces_along(piece, "k"):
            found.append((item, lambda a=place_y, b=place_k: a() * 2 + b()))
    return found


def solve(
    leaf_sides,
    leaf_inverse,
    leaf_panels,
    parent_map,
    tile_mask,
    top_sides,
    grand_inverse,
    child_inverse,
    root_inverse,
    child_panels,
    root_grand,
    root_child,
):
    owners = lax.axis_size("h")
    depth = lax.axis_size(DEPTH)
    part_rows = leaf_sides.shape[0]
    side_count = leaf_sides.shape[1]
    slice_rows = leaf_panels.shape[1]
    width = leaf_panels.shape[2]
    share_rows = top_sides.shape[1]
    half_rows = slice_rows // owners
    grand_rows = grand_inverse.shape[0]
    child_rows = child_inverse.shape[0]
    root_rows = root_inverse.shape[0]

    def of(matrix, pieces, name, **more):
        def product(starts, count, dtype):
            return times(matrix, pieces, starts, count, name=name, dtype=dtype, **more)

        return product

    parents = [parent_map] + others(parent_map, "h")
    root_near = shift(root_inverse, "g", 1)
    sides = panel_pieces(leaf_sides)

    def add_top(out_ref, slot, packet_refs, base):
        for step, packet_ref in enumerate(packet_refs):
            source = lax.axis_index(DEPTH) * owners + (lax.axis_index("h") - step) % owners

            @pl.when(source // depth == lax.axis_index("h"))
            def _():
                first = pl.multiple_of(base + source % depth * share_rows, share_rows)
                rows = pl.ds(first, share_rows)
                total = out_ref[rows, :].astype(F32) + packet_ref[slot].astype(F32)
                out_ref[rows, :] = total.astype(out_ref.dtype)

    leaf_lower = lower_held([leaf_inverse], [lambda: lax.axis_index(PANEL) * part_rows], lambda: 0)
    flags = spread_flags(tile_mask, slice_rows, side_count)
    panels = [loaded(leaf_panels, 0)]
    solved_leaf = times(leaf_lower, sides, [lambda: 0], part_rows, name="ls", dtype=BF16)
    all_solved = panel_pieces(solved_leaf)

    def panel_column():
        return lax.axis_index(PANEL) * slice_rows

    grand_lower = lower_held(
        [after(grand_inverse, solved_leaf)], [lambda: lax.axis_index("h") * grand_rows], panel_column,
    )
    packets = [top_sides] + others(top_sides, "h")
    kept, arrived = split_product(
        of(panels[0], all_solved, "gu", tiles=(flags, 0)), slice_rows, "h"
    )

    def slots_kernel(*refs):
        half_refs, packet_refs = refs[:owners], refs[owners : 2 * owners]
        parent_refs, out_refs = refs[2 * owners : 3 * owners], refs[3 * owners :]
        for step, out_ref in enumerate(out_refs):
            slot = lax.axis_index(DEPTH) ^ step
            total = jnp.zeros((half_rows, side_count), F32)
            for index, half_ref in enumerate(half_refs):
                chosen = (parent_refs[index][0] == slot).astype(F32)
                total = total - half_ref[...].astype(F32) * chosen
            out_ref[...] = total.astype(out_ref.dtype)
            add_top(out_ref, slot, packet_refs, 0)

    half_shape = (half_rows, side_count)
    slots = glue(
        slots_kernel,
        [(half_shape, F32)] + [(half_shape, BF16)] * (depth - 1),
        [kept] + arrived + packets,
        parents,
    )
    sent = slots[1:]
    arrived = [depth_shift(sent[step - 1], step) for step in range(1, depth)]

    late = [(after(piece, sent[0]), index) for piece, index in all_solved]
    panels += [loaded(leaf_panels, level) for level in (1, 2)]
    lower = [
        times(
            panels[level], late, [lambda: 0], slice_rows, name=f"lu{level}",
            tiles=(flags, level),
        )
        for level in (1, 2)
    ]

    def before_kernel(*refs):
        lower_refs, packet_refs = refs[:2], refs[2 : 2 + owners]
        parent_refs, out_refs = refs[2 + owners : 2 + 2 * owners], refs[2 + 2 * owners :]
        mine = (parent_refs[0][0] // 2 == lax.axis_index("c")).astype(F32)
        for step in range(owners):
            first = (lax.axis_index("h") + step) % owners * half_rows
            rows = lower_refs[0][pl.ds(pl.multiple_of(first, half_rows), half_rows), :]
            for weight, part in ((mine, 0), (1.0 - mine, 1)):
                window = pl.ds(part * half_rows, half_rows)
                out_refs[step][window, :] = (rows * -weight).astype(out_refs[step].dtype)
        add_top(out_refs[0], 4 + lax.axis_index("c"), packet_refs, 0)
        add_top(out_refs[0], 5 - lax.axis_index("c"), packet_refs, half_rows)
        out_refs[owners][...] = -lower_refs[1][...]
        add_top(out_refs[owners], 6, packet_refs, lax.axis_index("h") * half_rows)

    pair_shape = (2 * half_rows, side_count)
    before = glue(
        before_kernel,
        [(pair_shape, F32)]
        + [(pair_shape, BF16)] * (owners - 1)
        + [((slice_rows, side_count), F32)],
        lower + packets,
        parents,
    )
    root_before = before[owners]
    before_pair = total_of(before[0], [shift(before[step], "h", step) for step in range(1, owners)])
    grand_half_right = total_of(slots[0], arrived).astype(BF16)
    grand_right = pieces_along(grand_half_right, "h")
    child_before = before_pair[:half_rows] + shift(
        before_pair[half_rows:].astype(BF16), "c", 1
    ).astype(F32)

    child_lower = lower_held(
        [after(child_inverse, grand_half_right)],
        [lambda: (lax.axis_index("g") * owners + lax.axis_index("h")) * child_rows],
        panel_column,
    )

    def root_place(step):
        plane = lax.axis_index("c") * 2 + (lax.axis_index("g") + step) % 2
        return (plane * owners + lax.axis_index("h")) * root_rows

    grand_solved = panel_solve(of(grand_lower, grand_right, "gs"), grand_rows)

    kept, arrived = split_product(of(child_panels, grand_solved, "tc"), slice_rows, "h")
    root_before = times(
        root_grand, grand_solved, [lambda: 0], slice_rows, name="gr",
        plus=root_before, minus=True,
    )
    child_own = child_before - total_of(kept, arrived)
    child_right = total_of(child_own, others(child_own.astype(BF16), "g"))
    child_right = pieces_along(child_right.astype(BF16), "h")
    child_solved = panel_solve(of(child_lower, child_right, "cs"), child_rows)

    kept, arrived = split_product(
        of(root_child, child_solved, "tr", plus=root_before, minus=True), slice_rows, "h"
    )
    root_lower = lower_held(
        [after(root_inverse, child_right[0][0]), root_near],
        [lambda: root_place(0), lambda: root_place(1)],
        panel_column,
    )
    root_own = total_of(kept, arrived)
    root_own = total_of(root_own, others(root_own.astype(BF16), "g"))
    root_own = total_of(root_own, others(root_own.astype(BF16), "c"))
    root_right = pieces_along(root_own.astype(BF16), "h")
    root_solved = panel_solve(of(root_lower, root_right, "rs"), 2 * root_rows)
    root_own = total_of(
        *split_product(
            of(root_lower, root_solved, "rb", transposed=True), slice_rows, "h"
        )
    )
    root_half = total_of(root_own, others(root_own.astype(BF16), "c")).astype(BF16)
    root_result = pieces_along(root_half, "h")

    child_residual = panel_solve(
        of(root_child, root_result, "cb", transposed=True), child_rows, child_solved
    )
    grand_back = times(
        root_grand, root_result, [lambda: 0], grand_rows, name="rg", transposed=True
    )
    pulled = times(
        panels[2], root_result, [lambda: 0], width, name="rp", transposed=True,
        tiles=(flags, 2),
    )
    child_own = total_of(
        *split_product(
            of(child_lower, child_residual, "db", transposed=True), slice_rows, "h"
        )
    )
    child_half = total_of(child_own, others(child_own.astype(BF16), "g")).astype(BF16)
    child_result = pieces_along(child_half, "h")

    grand_residual = panel_solve(
        of(child_panels, child_result, "gb", transposed=True, plus=grand_back),
        grand_rows,
        grand_solved,
    )
    child_stack = jnp.stack([value for value, _ in child_result])
    child_other = shift(child_stack, "c", 1)
    kept, arrived = split_product(
        of(grand_lower, grand_residual, "eb", transposed=True), slice_rows, "h"
    )
    grand_half = total_of(kept, arrived).astype(BF16)

    grand_halves = [grand_half] + [depth_shift(grand_half, step) for step in range(1, depth)]

    def chosen_kernel(own_ref, other_ref, parent_ref, out_ref):
        mine = parent_ref[0] // 2 == lax.axis_index("c")

        @pl.when(mine)
        def _():
            out_ref[...] = own_ref[...]

        @pl.when(jnp.logical_not(mine))
        def _():
            out_ref[...] = other_ref[...]

    child_chosen = glue(
        chosen_kernel, [(child_stack.shape, BF16)], [child_stack, child_other], parents[:1]
    )[0]
    pulled = times(
        panels[1],
        [(child_chosen[step], index) for step, (_, index) in enumerate(child_result)],
        [lambda: 0],
        width,
        name="cp",
        transposed=True,
        tiles=(flags, 1),
        plus=pulled,
    )

    def results_kernel(*refs):
        half_refs, parent_refs = refs[:depth], refs[depth : depth + owners]
        mine_refs = refs[depth + owners : depth + 2 * owners]
        block_refs = refs[depth + 2 * owners :]
        for step in range(depth):
            slot = lax.axis_index(DEPTH) ^ step
            for index in range(owners):

                @pl.when(parent_refs[(owners - index) % owners][0] == slot)
                def _():
                    mine_refs[index][...] = half_refs[step][...]

                target = lax.axis_index(DEPTH) * owners + (lax.axis_index("h") + index) % owners
                first = pl.multiple_of(target % depth * share_rows, share_rows)
                block_refs[index][slot] = half_refs[step][pl.ds(first, share_rows), :]

    block_shape = (depth, share_rows, side_count)
    results = glue(
        results_kernel,
        [(half_shape, BF16)] * owners + [(block_shape, BF16)] * owners,
        grand_halves,
        parents,
    )
    blocks = results[owners:]
    grand_mine = [(results[0], lambda: lax.axis_index("h"))]
    for step in range(1, owners):
        grand_mine.append(
            (
                shift(results[step], "h", step),
                lambda step=step: (lax.axis_index("h") - step) % owners,
            )
        )

    leaf_pulled = panel_split(
        of(panels[0], grand_mine, "gp", transposed=True, tiles=(flags, 0), plus=pulled), width
    )
    leaf_residual = (solved_leaf.astype(F32) - leaf_pulled).astype(BF16)

    arrived = [blocks[0]] + [shift(blocks[step], "h", step) for step in range(1, owners)]

    def tops_kernel(*refs):
        block_refs, root_refs = refs[:owners], refs[owners : 2 * owners]
        child_refs = refs[2 * owners : 2 * owners + 2]
        out_ref = refs[-1]
        holder = lax.axis_index(LEAF) // depth
        rows = pl.ds(
            pl.multiple_of(lax.axis_index(LEAF) % depth * share_rows, share_rows), share_rows
        )
        for step in range(owners):

            @pl.when((lax.axis_index("h") - step) % owners == holder)
            def _():
                out_ref[0:depth] = block_refs[step][...]
                out_ref[4 + lax.axis_index("c")] = child_refs[0][step, rows, :]
                out_ref[5 - lax.axis_index("c")] = child_refs[1][step, rows, :]
                out_ref[6] = root_refs[step][rows, :]

    top_solution = glue(
        tops_kernel,
        [((7, share_rows, side_count), BF16)],
        arrived + [value for value, _ in root_result] + [child_stack, child_other],
        [],
    )[0]
    leaf_solution = panel_split(
        of(leaf_lower, own(leaf_residual), "lb", transposed=True), width
    ).astype(BF16)
    return leaf_solution, top_solution


def solution(mesh):
    leaf_count = mesh.shape["leaf"]
    panel_count = mesh.shape["panel"]
    split_mesh = Mesh(
        mesh.devices.reshape(2, 2, leaf_count // 4, panel_count // 2, 2), LEAF + PANEL
    )
    placed = (
        P(LEAF + PANEL, None),
        P(LEAF + PANEL, None),
        P(None, PANEL, LEAF),
        P(LEAF),
        P(LEAF, None, None),
        P(None, PANEL + LEAF, None),
        P(LEAF, PANEL),
        P(LEAF, PANEL),
        P(LEAF, PANEL),
        P(PANEL, LEAF),
        P(PANEL, LEAF),
        P(PANEL, LEAF),
    )
    return jax.shard_map(
        solve,
        mesh=split_mesh,
        in_specs=placed,
        out_specs=(P(LEAF + PANEL, None), P(None, PANEL + LEAF, None)),
        check_vma=False,
    )
```

```python
import jax
import jax.numpy as jnp
from jax import lax
from jax.experimental import pallas as pl
from jax.experimental.pallas import tpu as pltpu
from jax.sharding import Mesh
from jax.sharding import PartitionSpec as P


TILE_ROWS = 128
LANES = 128
LEAF = ("c", "g", "h")
PANEL = ("y", "k")
DEPTH = ("c", "g")
ROWS = ("h", "g")
F32 = jnp.float32
BF16 = jnp.bfloat16
VMEM = pltpu.VMEM


def after(value, other):
    return lax.optimization_barrier((value, other))[0]


def lower_part(matrix, row_offset, col_offset):
    row_index = row_offset + lax.broadcasted_iota(jnp.int32, matrix.shape, 0)
    col_index = col_offset + lax.broadcasted_iota(jnp.int32, matrix.shape, 1)
    return jnp.where(row_index >= col_index, matrix, jnp.zeros_like(matrix))


def rows_at(value, start, count, axis=0):
    starts = [jnp.int32(0)] * value.ndim
    starts[axis] = start
    sizes = list(value.shape)
    sizes[axis] = count
    return lax.dynamic_slice(value, starts, sizes, allow_negative_indices=False)


def own(value):
    return [(value, lambda: 0)]


def joined(pieces):
    if len(pieces) == 1:
        return pieces[0][0]
    count = pieces[0][0].shape[0]
    place = lax.broadcasted_iota(jnp.int32, (len(pieces),) + pieces[0][0].shape, 0)
    whole = jnp.broadcast_to(pieces[0][0][None], place.shape)
    for value, index in pieces[1:]:
        whole = jnp.where(place == index(), value[None], whole)
    return whole.reshape((len(pieces) * count,) + pieces[0][0].shape[1:])


def loaded(matrices, level):
    rows, columns = matrices.shape[1:]
    parts = 4

    def kernel(from_ref, out_ref, sems):
        copies = []
        for part in range(parts):
            window = pl.ds(part * (rows // parts), rows // parts)
            copy = pltpu.make_async_copy(
                from_ref.at[level, window], out_ref.at[window], sems.at[part]
            )
            copy.start()
            copies.append(copy)
        for copy in copies:
            copy.wait()

    return pl.pallas_call(
        kernel,
        out_shape=jax.ShapeDtypeStruct((rows, columns), matrices.dtype),
        in_specs=[pl.BlockSpec(memory_space=pltpu.HBM)],
        out_specs=pl.BlockSpec(memory_space=VMEM),
        scratch_shapes=[pltpu.SemaphoreType.DMA((parts,))],
        compiler_params=pltpu.CompilerParams(vmem_limit_bytes=5 << 20),
        cost_estimate=pl.CostEstimate(
            flops=0, bytes_accessed=2 * rows * columns, transcendentals=0
        ),
        name="lp",
    )(pltpu.with_memory_space_constraint(matrices, pltpu.HBM))


def spread_flags(tile_mask, rows, sides):
    def kernel(flag_ref, out_ref):
        tile = lax.axis_index(PANEL) * (rows // TILE_ROWS)
        for level in range(3):
            for part in range(rows // TILE_ROWS):
                flag = flag_ref[0, level, tile + part].astype(F32)
                out_ref[level, part * TILE_ROWS : (part + 1) * TILE_ROWS, :] = jnp.full(
                    (TILE_ROWS, sides), flag, F32
                ).astype(BF16)

    return pl.pallas_call(
        kernel,
        out_shape=jax.ShapeDtypeStruct((3, rows, sides), BF16),
        in_specs=[pl.BlockSpec(memory_space=pltpu.SMEM)],
        out_specs=pl.BlockSpec(memory_space=VMEM),
        compiler_params=pltpu.CompilerParams(vmem_limit_bytes=2 << 20),
        name="fl",
    )(tile_mask)


def lower_held(blocks, row_places, column_place):
    rows, columns = blocks[0].shape
    chunk = min(rows, 256)
    count = rows // chunk

    def kernel(*refs):
        out_ref, sems = refs[-2], refs[-1]
        copies = []
        for index in range(len(blocks)):
            for part in range(count):
                copy = pltpu.make_async_copy(
                    refs[index].at[pl.ds(part * chunk, chunk)],
                    out_ref.at[pl.ds((index * count + part) * chunk, chunk)],
                    sems.at[index * count + part],
                )
                copy.start()
                copies.append(copy)
        first_column = column_place()
        for index, row_place in enumerate(row_places):
            for part in range(count):
                copies[index * count + part].wait()
                window = pl.ds((index * count + part) * chunk, chunk)
                first_row = row_place() + part * chunk
                clear = first_row + chunk <= first_column

                @pl.when(clear)
                def _():
                    out_ref[window, :] = jnp.zeros((chunk, columns), BF16)

                @pl.when(jnp.logical_not(clear) & (first_row < first_column + columns - 1))
                def _():
                    out_ref[window, :] = lower_part(out_ref[window, :], first_row, first_column)

    return pl.pallas_call(
        kernel,
        out_shape=jax.ShapeDtypeStruct((len(blocks) * rows, columns), BF16),
        in_specs=[pl.BlockSpec(memory_space=pltpu.HBM)] * len(blocks),
        out_specs=pl.BlockSpec(memory_space=VMEM),
        scratch_shapes=[pltpu.SemaphoreType.DMA((len(blocks) * count,))],
        compiler_params=pltpu.CompilerParams(vmem_limit_bytes=4 << 20),
        cost_estimate=pl.CostEstimate(
            flops=0, bytes_accessed=2 * len(blocks) * rows * columns, transcendentals=0
        ),
    )(*[pltpu.with_memory_space_constraint(block, pltpu.HBM) for block in blocks])


def times(
    matrix, pieces, starts, count, *, name, transposed=False, plus=None, minus=False,
    tiles=None, dtype=F32,
):
    if pieces[0][0].shape[0] % LANES:
        pieces = own(joined(pieces))
    full = matrix.shape[int(transposed)]
    if count % LANES and count < full:
        whole = times(
            matrix, pieces, [lambda: 0], full, name=name, transposed=transposed, plus=plus,
            minus=minus, tiles=tiles, dtype=dtype,
        )
        return jnp.concatenate([rows_at(whole, start(), count) for start in starts], axis=0)
    width = pieces[0][0].shape[0]
    sides = pieces[0][0].shape[1]
    extra = [] if plus is None else [plus]
    flags = [] if tiles is None else [tiles[0]]

    def place(value):
        return pl.multiple_of(value, LANES)

    def kernel(matrix_ref, *refs):
        out_ref = refs[-1]
        vector_refs = refs[: len(pieces)]
        plus_ref = refs[len(pieces)]
        flag_ref = refs[-2]

        vectors = []
        for vector_ref, (_, index) in zip(vector_refs, pieces):
            first = place(index() * width)
            vector = vector_ref[...]
            if tiles is not None and transposed:
                vector = vector * flag_ref[tiles[1], pl.ds(first, width), :]
            vectors.append((vector, pl.ds(first, width)))
        for step, start in enumerate(starts):
            first = place(start()) if count < full else 0
            window = pl.ds(first, count)
            total = None
            for vector, rows in vectors:
                if transposed:
                    part = lax.dot_general(
                        vector,
                        matrix_ref[rows, window],
                        (((0,), (0,)), ((), ())),
                        preferred_element_type=F32,
                    )
                else:
                    part = jnp.dot(
                        matrix_ref[window, rows], vector, preferred_element_type=F32
                    )
                total = part if total is None else total + part
            if transposed:
                total = total.T
            if tiles is not None and not transposed:
                total = total * flag_ref[tiles[1], window, :].astype(F32)
            if plus is not None:
                before = plus_ref[window, :].astype(F32)
                total = before - total if minus else before + total
            out_ref[pl.ds(step * count, count), :] = total.astype(dtype)

    depth = len(pieces) * width
    return pl.pallas_call(
        kernel,
        out_shape=jax.ShapeDtypeStruct((len(starts) * count, sides), dtype),
        in_specs=[pl.BlockSpec(memory_space=VMEM)] * (1 + len(pieces) + len(extra) + len(flags)),
        out_specs=pl.BlockSpec(memory_space=VMEM),
        compiler_params=pltpu.CompilerParams(vmem_limit_bytes=8 << 20),
        cost_estimate=pl.CostEstimate(
            flops=2 * len(starts) * count * depth * sides,
            bytes_accessed=2 * len(starts) * count * depth,
            transcendentals=0,
        ),
    )(matrix, *[value for value, _ in pieces], *extra, *flags)


def glue(kernel, outs, vectors, parents):
    return pl.pallas_call(
        kernel,
        out_shape=[jax.ShapeDtypeStruct(shape, dtype) for shape, dtype in outs],
        in_specs=[pl.BlockSpec(memory_space=VMEM)] * len(vectors)
        + [pl.BlockSpec(memory_space=pltpu.SMEM)] * len(parents),
        out_specs=[pl.BlockSpec(memory_space=VMEM)] * len(outs),
        compiler_params=pltpu.CompilerParams(vmem_limit_bytes=6 << 20),
        cost_estimate=pl.CostEstimate(
            flops=0, bytes_accessed=sum(2 * value.size for value in vectors), transcendentals=0
        ),
    )(*vectors, *parents)


def place_on(axis):
    if axis == ROWS:
        return lax.axis_index("h") * lax.axis_size("g") + lax.axis_index("g")
    return lax.axis_index(axis)


def shift(value, axis, step):
    size = lax.axis_size(axis)
    pairs = [(i, i ^ step) for i in range(size)]
    along = axis
    if axis == ROWS:
        along = ROWS[::-1]
        slow, fast = lax.axis_size("h"), lax.axis_size("g")
        pairs = [tuple(i % fast * slow + i // fast for i in pair) for pair in pairs]
    return lax.ppermute(value, along, pairs)


def others(value, axis):
    return [shift(value, axis, step) for step in range(1, lax.axis_size(axis))]


def pieces_along(value, axis):
    found = [(value, lambda: place_on(axis))]
    for step, piece in enumerate(others(value, axis), 1):
        found.append((piece, lambda step=step: place_on(axis) ^ step))
    return found


def split_product(product, count, axis):
    size = lax.axis_size(axis)
    block = count // size
    arrived = []
    for step in range(1, size):
        sent = product([lambda step=step: (place_on(axis) ^ step) * block], block, BF16)
        arrived.append(shift(sent, axis, step))
    kept = product([lambda: place_on(axis) * block], block, F32)
    return kept, arrived


def total_of(kept, arrived):
    for part in arrived:
        kept = kept + part.astype(F32)
    return kept


def panel_solve(product, count, less_from=None):
    half = total_of(*split_product(product, count, "k"))
    half = total_of(half, others(half.astype(BF16), "y"))
    if less_from is not None:
        half = less_from[0][0].astype(F32) - half
    return pieces_along(half.astype(BF16), "k")


def panel_split(product, count):
    rows_y = lax.axis_size("y")
    block = count // rows_y // 2

    def blocks_of(core, dtype):
        starts = [
            lambda step=step: (
                (lax.axis_index("y") ^ step) * 2 + (lax.axis_index("k") ^ core)
            ) * block
            for step in range(rows_y)
        ]
        return product(starts, block, dtype)

    sent = shift(blocks_of(1, BF16), "k", 1)
    sums = blocks_of(0, F32) + sent.astype(F32)
    total = sums[:block]
    for step in range(1, rows_y):
        moved = sums[step * block : (step + 1) * block].astype(BF16)
        total = total + shift(moved, "y", step).astype(F32)
    return total


def depth_shift(value, step):
    size = lax.axis_size(DEPTH)
    return lax.ppermute(value, DEPTH, [(i, i ^ step) for i in range(size)])


def panel_pieces(value):
    found = []
    for piece, place_y in pieces_along(value, "y"):
        for item, place_k in pieces_along(piece, "k"):
            found.append((item, lambda a=place_y, b=place_k: a() * 2 + b()))
    return found


def solve(
    leaf_sides,
    leaf_inverse,
    leaf_panels,
    parent_map,
    tile_mask,
    top_sides,
    grand_inverse,
    child_inverse,
    root_inverse,
    child_panels,
    root_grand,
    root_child,
):
    owners = lax.axis_size("h")
    depth = lax.axis_size(DEPTH)
    part_rows = leaf_sides.shape[0]
    side_count = leaf_sides.shape[1]
    slice_rows = leaf_panels.shape[1]
    width = leaf_panels.shape[2]
    share_rows = top_sides.shape[1]
    half_rows = slice_rows // owners
    grand_rows = grand_inverse.shape[0]
    child_rows = child_inverse.shape[0]
    root_rows = root_inverse.shape[0]

    def of(matrix, pieces, name, **more):
        def product(starts, count, dtype):
            return times(matrix, pieces, starts, count, name=name, dtype=dtype, **more)

        return product

    parents = [parent_map] + others(parent_map, "h")
    root_near = shift(root_inverse, "g", 1)
    sides = panel_pieces(leaf_sides)

    def add_top(out_ref, slot, packet_refs, base):
        for step, packet_ref in enumerate(packet_refs):
            source = lax.axis_index(DEPTH) * owners + (lax.axis_index("h") ^ step)

            @pl.when(source // depth == lax.axis_index("h"))
            def _():
                first = pl.multiple_of(base + source % depth * share_rows, share_rows)
                rows = pl.ds(first, share_rows)
                total = out_ref[rows, :].astype(F32) + packet_ref[slot].astype(F32)
                out_ref[rows, :] = total.astype(out_ref.dtype)

    leaf_lower = lower_held([leaf_inverse], [lambda: lax.axis_index(PANEL) * part_rows], lambda: 0)
    flags = spread_flags(tile_mask, slice_rows, side_count)
    panels = [loaded(leaf_panels, 0)]
    solved_leaf = times(leaf_lower, sides, [lambda: 0], part_rows, name="ls", dtype=BF16)
    all_solved = panel_pieces(solved_leaf)

    def panel_column():
        return lax.axis_index(PANEL) * slice_rows

    grand_lower = lower_held(
        [after(grand_inverse, solved_leaf)], [lambda: lax.axis_index("h") * grand_rows], panel_column,
    )
    packets = [top_sides] + others(top_sides, "h")
    kept, arrived = split_product(
        of(panels[0], all_solved, "gu", tiles=(flags, 0)), slice_rows, "h"
    )

    def slots_kernel(*refs):
        half_refs, packet_refs = refs[:owners], refs[owners : 2 * owners]
        parent_refs, out_refs = refs[2 * owners : 3 * owners], refs[3 * owners :]
        for step, out_ref in enumerate(out_refs):
            slot = lax.axis_index(DEPTH) ^ step
            total = jnp.zeros((half_rows, side_count), F32)
            for index, half_ref in enumerate(half_refs):
                chosen = (parent_refs[index][0] == slot).astype(F32)
                total = total - half_ref[...].astype(F32) * chosen
            out_ref[...] = total.astype(out_ref.dtype)
            add_top(out_ref, slot, packet_refs, 0)

    half_shape = (half_rows, side_count)
    slots = glue(
        slots_kernel,
        [(half_shape, F32)] + [(half_shape, BF16)] * (depth - 1),
        [kept] + arrived + packets,
        parents,
    )
    sent = slots[1:]
    arrived = [depth_shift(sent[step - 1], step) for step in range(1, depth)]

    late = [(after(piece, sent[0]), index) for piece, index in all_solved]
    panels += [loaded(leaf_panels, level) for level in (1, 2)]
    lower = [
        times(
            panels[level], late, [lambda: 0], slice_rows, name=f"lu{level}",
            tiles=(flags, level),
        )
        for level in (1, 2)
    ]

    def before_kernel(*refs):
        lower_refs, packet_refs = refs[:2], refs[2 : 2 + owners]
        parent_refs, out_refs = refs[2 + owners : 2 + 2 * owners], refs[2 + 2 * owners :]
        mine = (parent_refs[0][0] // 2 == lax.axis_index("c")).astype(F32)
        for step in range(owners):
            first = (lax.axis_index("h") ^ step) * half_rows
            rows = lower_refs[0][pl.ds(pl.multiple_of(first, half_rows), half_rows), :]
            for weight, part in ((mine, 0), (1.0 - mine, 1)):
                window = pl.ds(part * half_rows, half_rows)
                out_refs[step][window, :] = (rows * -weight).astype(out_refs[step].dtype)
        add_top(out_refs[0], 4 + lax.axis_index("c"), packet_refs, 0)
        add_top(out_refs[0], 5 - lax.axis_index("c"), packet_refs, half_rows)
        out_refs[owners][...] = -lower_refs[1][...]
        add_top(out_refs[owners], 6, packet_refs, lax.axis_index("h") * half_rows)

    quarter = half_rows // 2
    pair_shape = (2 * half_rows, side_count)
    before = glue(
        before_kernel,
        [(pair_shape, F32)]
        + [(pair_shape, BF16)] * (owners - 1)
        + [((slice_rows, side_count), F32)],
        lower + packets,
        parents,
    )
    root_before = before[owners]

    def quarters_kernel(*refs):
        kept_ref, sent_ref = refs[-2:]
        for part in range(2):
            for step, out_ref in enumerate((kept_ref, sent_ref)):
                first = part * half_rows + (lax.axis_index("g") ^ step) * quarter
                rows = pl.ds(pl.multiple_of(first, quarter), quarter)
                total = refs[0][rows, :]
                for found_ref in refs[1:-2]:
                    total = total + found_ref[rows, :].astype(F32)
                out_ref[part * quarter : (part + 1) * quarter, :] = total.astype(out_ref.dtype)

    quarters = glue(
        quarters_kernel,
        [((half_rows, side_count), F32), ((half_rows, side_count), BF16)],
        [before[0]] + [shift(before[step], "h", step) for step in range(1, owners)],
        [],
    )
    before_pair = total_of(quarters[0], [shift(quarters[1], "g", 1)])
    grand_half_right = total_of(slots[0], arrived).astype(BF16)
    grand_right = pieces_along(grand_half_right, "h")
    child_before = before_pair[:quarter] + shift(
        before_pair[quarter:].astype(BF16), "c", 1
    ).astype(F32)

    child_lower = lower_held(
        [after(child_inverse, grand_half_right)],
        [lambda: (lax.axis_index("g") * owners + lax.axis_index("h")) * child_rows],
        panel_column,
    )

    def root_place(step):
        plane = lax.axis_index("c") * 2 + (lax.axis_index("g") + step) % 2
        return (plane * owners + lax.axis_index("h")) * root_rows

    grand_solved = panel_solve(of(grand_lower, grand_right, "gs"), grand_rows)

    kept, arrived = split_product(of(child_panels, grand_solved, "tc"), slice_rows, ROWS)
    root_before = times(
        root_grand, grand_solved, [lambda: 0], slice_rows, name="gr",
        plus=root_before, minus=True,
    )
    child_own = child_before - total_of(kept, arrived)
    child_right = pieces_along(child_own.astype(BF16), ROWS)
    child_solved = panel_solve(of(child_lower, child_right, "cs"), child_rows)

    kept, arrived = split_product(
        of(root_child, child_solved, "tr", plus=root_before, minus=True), slice_rows, ROWS
    )
    root_lower = lower_held(
        [after(root_inverse, child_right[0][0]), root_near],
        [lambda: root_place(0), lambda: root_place(1)],
        panel_column,
    )
    root_own = total_of(kept, arrived)
    root_own = total_of(root_own, others(root_own.astype(BF16), "c"))
    root_right = pieces_along(root_own.astype(BF16), ROWS)
    root_solved = panel_solve(of(root_lower, root_right, "rs"), 2 * root_rows)
    arrived = []
    back = of(root_lower, root_solved, "rb", transposed=True)

    def root_start(step):
        return lambda: (lax.axis_index("h") ^ step) * half_rows + lax.axis_index("g") * quarter

    for step in range(1, owners):
        arrived.append(shift(back([root_start(step)], quarter, BF16), "h", step))
    root_own = total_of(back([root_start(0)], quarter, F32), arrived)
    root_own = total_of(root_own, others(root_own.astype(BF16), "c")).astype(BF16)
    root_result = pieces_along(root_own, ROWS)

    child_residual = panel_solve(
        of(root_child, root_result, "cb", transposed=True), child_rows, child_solved
    )
    grand_back = times(
        root_grand, root_result, [lambda: 0], grand_rows, name="rg", transposed=True
    )
    pulled = times(
        panels[2], root_result, [lambda: 0], width, name="rp", transposed=True,
        tiles=(flags, 2),
    )
    child_own = total_of(
        *split_product(
            of(child_lower, child_residual, "db", transposed=True), slice_rows, ROWS
        )
    )
    child_result = pieces_along(child_own.astype(BF16), ROWS)

    grand_residual = panel_solve(
        of(child_panels, child_result, "gb", transposed=True, plus=grand_back),
        grand_rows,
        grand_solved,
    )
    child_stack = jnp.stack([value for value, _ in child_result])
    child_other = shift(child_stack, "c", 1)
    kept, arrived = split_product(
        of(grand_lower, grand_residual, "eb", transposed=True), slice_rows, "h"
    )
    grand_half = total_of(kept, arrived).astype(BF16)

    grand_halves = [grand_half] + [depth_shift(grand_half, step) for step in range(1, depth)]

    def chosen_kernel(own_ref, other_ref, parent_ref, out_ref):
        mine = parent_ref[0] // 2 == lax.axis_index("c")

        @pl.when(mine)
        def _():
            out_ref[...] = own_ref[...]

        @pl.when(jnp.logical_not(mine))
        def _():
            out_ref[...] = other_ref[...]

    child_chosen = glue(
        chosen_kernel, [(child_stack.shape, BF16)], [child_stack, child_other], parents[:1]
    )[0]
    pulled = times(
        panels[1],
        [(child_chosen[step], index) for step, (_, index) in enumerate(child_result)],
        [lambda: 0],
        width,
        name="cp",
        transposed=True,
        tiles=(flags, 1),
        plus=pulled,
    )

    def results_kernel(*refs):
        half_refs, parent_refs = refs[:depth], refs[depth : depth + owners]
        mine_refs = refs[depth + owners : depth + 2 * owners]
        block_refs = refs[depth + 2 * owners :]
        for step in range(depth):
            slot = lax.axis_index(DEPTH) ^ step
            for index in range(owners):

                @pl.when(parent_refs[index][0] == slot)
                def _():
                    mine_refs[index][...] = half_refs[step][...]

                target = lax.axis_index(DEPTH) * owners + (lax.axis_index("h") ^ index)
                first = pl.multiple_of(target % depth * share_rows, share_rows)
                block_refs[index][slot] = half_refs[step][pl.ds(first, share_rows), :]

    block_shape = (depth, share_rows, side_count)
    results = glue(
        results_kernel,
        [(half_shape, BF16)] * owners + [(block_shape, BF16)] * owners,
        grand_halves,
        parents,
    )
    blocks = results[owners:]
    grand_mine = [(results[0], lambda: lax.axis_index("h"))]
    for step in range(1, owners):
        grand_mine.append(
            (
                shift(results[step], "h", step),
                lambda step=step: lax.axis_index("h") ^ step,
            )
        )

    leaf_pulled = panel_split(
        of(panels[0], grand_mine, "gp", transposed=True, tiles=(flags, 0), plus=pulled), width
    )
    leaf_residual = (solved_leaf.astype(F32) - leaf_pulled).astype(BF16)

    arrived = [blocks[0]] + [shift(blocks[step], "h", step) for step in range(1, owners)]

    def tops_kernel(*refs):
        block_refs, root_refs = refs[:owners], refs[owners : 3 * owners]
        child_refs = refs[3 * owners : 3 * owners + 2]
        out_ref = refs[-1]
        place = lax.axis_index(LEAF)
        for step in range(owners):

            @pl.when(lax.axis_index("h") ^ step == place // depth)
            def _():
                out_ref[0:depth] = block_refs[step][...]

        rows = pl.ds(pl.multiple_of(place % 2 * share_rows, share_rows), share_rows)
        for step in range(2 * owners):

            @pl.when(place_on(ROWS) ^ step == place // 2)
            def _():
                out_ref[4 + lax.axis_index("c")] = child_refs[0][step, rows, :]
                out_ref[5 - lax.axis_index("c")] = child_refs[1][step, rows, :]
                out_ref[6] = root_refs[step][rows, :]

    top_solution = glue(
        tops_kernel,
        [((7, share_rows, side_count), BF16)],
        arrived + [value for value, _ in root_result] + [child_stack, child_other],
        [],
    )[0]
    leaf_solution = panel_split(
        of(leaf_lower, own(leaf_residual), "lb", transposed=True), width
    ).astype(BF16)
    return leaf_solution, top_solution


def solution(mesh):
    leaf_count = mesh.shape["leaf"]
    panel_count = mesh.shape["panel"]
    split_mesh = Mesh(
        mesh.devices.reshape(2, 2, leaf_count // 4, panel_count // 2, 2), LEAF + PANEL
    )
    placed = (
        P(LEAF + PANEL, None),
        P(LEAF + PANEL, None),
        P(None, PANEL, LEAF),
        P(LEAF),
        P(LEAF, None, None),
        P(None, PANEL + LEAF, None),
        P(LEAF, PANEL),
        P(LEAF, PANEL),
        P(LEAF, PANEL),
        P(PANEL, LEAF),
        P(PANEL, LEAF),
        P(PANEL, LEAF),
    )
    return jax.shard_map(
        solve,
        mesh=split_mesh,
        in_specs=placed,
        out_specs=(P(LEAF + PANEL, None), P(None, PANEL + LEAF, None)),
        check_vma=False,
    )
```
